256 devices in a mesh: space: 8 (over z_lo, y), vec: 32 (over x, z_hi, core).
Axes of the slice: x: 4, y: 4, z: 8 (z_hi: 4, z_lo: 2; z = z_hi * 2 + z_lo), core: 2. Of those that a mesh axis runs over, the one named last changes fastest.
Arguments:
- vectors: float32 [2, 3, 128, 8, 4096], P(None, None, 'vec', 'space'), may hold values from -6 to 6
- gauge_links: float32 [3, 2, 3, 3, 8, 4096], P(None, None, None, None, 'space'), may hold values from -2.5 to 2.5
- momenta: int32 [2, 3], replicated, may hold values from 1 to 2
- displacements: int32 [2], replicated, may hold values from 0 to 5
Outputs:
- elementals: float32 [2, 4, 128, 128], P(None, None, 'vec', 'space')
The draws below stay inside these ranges and needn't reach their ends.
All inputs are finite; a program needn't handle non-finite values.
Results may differ from the reference program's by a relative error of at most 0.0003.
Values sent between devices are 32-bit elements; how exact they have to be, the bound alone decides.
No kernel may reach another device: no remote copies, remote signals or barrier semaphores. Data moves between devices by JAX's collectives and lax.ppermute only.
A program may use at most 128 MiB of HBM per device.

```python
import math
from functools import partial
import jax
import jax.numpy as jnp
from jax import lax

NY = 64
NZ = 64
NVEC = 128
NMOM = 2
NDISP = 2
NX = 8


def with_ends(values, stream_key, low, largest):
    longest = values.shape.index(max(values.shape))
    spots = []
    for shift in (0, 1):
        where = [jax.random.randint(jax.random.fold_in(stream_key, axis), (), 0, length) for axis, length in enumerate(values.shape)]
        where[longest] = (where[longest] + shift) % values.shape[longest]
        spots.append(tuple(where))
    return values.at[spots[0]].set(low).at[spots[1]].set(largest)


def block_scale(key, extent, cuts, smallest, top_value):
    level = 1.0
    for position, shards_of in cuts:
        draws = jax.random.uniform(jax.random.fold_in(jax.random.fold_in(key, 6), position), (shards_of,), jnp.float32, smallest / len(cuts), top_value / len(cuts))
        level = level * jnp.repeat(jnp.exp(draws), extent[position] // shards_of).reshape((-1,) + (1,) * (len(extent) - 1 - position))
    return level


def normal_values(rng, shape, width, most, split=(), kind=jnp.bfloat16):
    result = jax.random.normal(rng, shape, jnp.float32) * width
    if len(split) > 0:
        result = block_scale(rng, shape, split, -0.22, 0.18) * result
    return jnp.clip(result, min=-most, max=most).astype(kind)


def setup_inputs(seed: int = 0) -> dict:
    arg_keys = jax.random.split(jax.random.key(seed), 5)
    return {
        "vectors": normal_values(arg_keys[0], (2, 3, NVEC, NX, NY * NZ), 1.0, 6.0, ((2, 32), (3, 8)), jnp.float32),
        "gauge_links": normal_values(arg_keys[1], (3, 2, 3, 3, NX, NY * NZ), 0.4, 2.5, ((4, 8),), jnp.float32),
        "momenta": with_ends(jax.random.randint(arg_keys[2], (NMOM, 3), 1, 3), jax.random.fold_in(arg_keys[2], 1), 1, 2).astype(jnp.int32),
        "displacements": jax.random.randint(arg_keys[3], (NDISP,), 0, 6).astype(jnp.int32),
    }


def colour_term(gauge_one, colour_field, colour, dagger):
    if dagger:
        link_re = gauge_one[0][colour][:, None]
        link_im = -gauge_one[1][colour][:, None]
    else:
        link_re = gauge_one[0][:, colour][:, None]
        link_im = gauge_one[1][:, colour][:, None]
    vec_re = colour_field[0][colour][None]
    vec_im = colour_field[1][colour][None]
    return (link_re * vec_re - link_im * vec_im, link_re * vec_im + link_im * vec_re)

def link_times(gauge_one, colour_field, dagger):
    real_sum, imag_sum = colour_term(gauge_one, colour_field, 0, dagger)
    for colour in (1, 2):
        real_next, imag_next = colour_term(gauge_one, colour_field, colour, dagger)
        real_sum = real_sum + real_next
        imag_sum = imag_sum + imag_next
    return jnp.stack([real_sum, imag_sum])

def single_hop(colour_field, gauge_sites, hop_index):
    direction = hop_index % 3
    spatial_axis = 3 + direction
    if hop_index < 3:
        return link_times(gauge_sites[direction], jnp.roll(colour_field, -1, spatial_axis), False)
    return jnp.roll(link_times(gauge_sites[direction], colour_field, True), 1, spatial_axis)

def hopping(colour_field, gauge_sites):
    running = single_hop(colour_field, gauge_sites, 0)
    for hop_index in range(1, 6):
        running = running + single_hop(colour_field, gauge_sites, hop_index)
    return running

def pair_sums(left_side, right_side):
    hig = lax.Precision.HIGHEST
    real_part = jnp.einsum('cixyz,cjxyz->ij', left_side[0], right_side[0], precision=hig) + jnp.einsum('cixyz,cjxyz->ij', left_side[1], right_side[1], precision=hig)
    imag_part = jnp.einsum('cixyz,cjxyz->ij', left_side[0], right_side[1], precision=hig) - jnp.einsum('cixyz,cjxyz->ij', left_side[1], right_side[0], precision=hig)
    return (real_part, imag_part)

def reference(vectors, gauge_links, momenta, displacements):
    global_planes = vectors.shape[3]
    start_field = vectors.reshape(2, 3, NVEC, global_planes, NY, NZ)
    gauge_sites = gauge_links.reshape(3, 2, 3, 3, global_planes, NY, NZ)
    first_step = hopping(start_field, gauge_sites) / -6.0
    filtered = hopping(first_step, gauge_sites) / -3.0 - start_field
    plane_index = jnp.arange(global_planes, dtype=jnp.int32)
    row_index = jnp.arange(NY, dtype=jnp.int32)
    depth_index = jnp.arange(NZ, dtype=jnp.int32)
    real_rows = []
    imag_rows = []
    for op_index in range(NMOM):
        phase_plane = (momenta[op_index, 0] * plane_index % global_planes).astype(jnp.float32) / global_planes
        phase_row = (momenta[op_index, 1] * row_index % NY).astype(jnp.float32) / NY
        phase_depth = (momenta[op_index, 2] * depth_index % NZ).astype(jnp.float32) / NZ
        angle_grid = (phase_plane[:, None, None] + phase_row[None, :, None] + phase_depth[None, None, :]) * (2.0 * math.pi)
        cosine = jnp.cos(angle_grid)
        sine_part = jnp.sin(angle_grid)
        phased = jnp.stack([cosine * filtered[0] - sine_part * filtered[1], cosine * filtered[1] + sine_part * filtered[0]])
        real_part, imag_part = pair_sums(filtered, phased)
        real_rows.append(real_part)
        imag_rows.append(imag_part)
    branches = [partial(single_hop, hop_index=hop_index) for hop_index in range(6)]
    for op_index in range(NDISP):
        displaced = lax.switch(displacements[op_index], branches, filtered, gauge_sites)
        real_part, imag_part = pair_sums(filtered, displaced)
        real_rows.append(real_part)
        imag_rows.append(imag_part)
    norm_scale = 1.0 / math.sqrt(3 * global_planes * NY * NZ)
    return jnp.stack([jnp.stack(real_rows), jnp.stack(imag_rows)]) * norm_scale
```

```python
import functools
import math

import jax
import jax.numpy as jnp
from jax import lax
from jax.experimental import pallas as pl
from jax.experimental.pallas import tpu as pltpu
from jax.sharding import PartitionSpec as P

NY = 64
NZ = 64
NMOM = 2
NDISP = 2
ROWS = 32
LANES = 128
VMEM = pltpu.VMEM
F32 = jnp.float32


def call(body, out_shape, n_in, scratch=(), scalars=False, flops=0, nbytes=0):
    specs = [pl.BlockSpec(memory_space=VMEM)] * n_in
    if scalars:
        specs = [pl.BlockSpec(memory_space=pltpu.SMEM)] + specs
    many = isinstance(out_shape, (list, tuple))
    return pl.pallas_call(
        body,
        out_shape=out_shape,
        in_specs=specs,
        out_specs=[pl.BlockSpec(memory_space=VMEM)] * len(out_shape)
        if many
        else pl.BlockSpec(memory_space=VMEM),
        scratch_shapes=list(scratch),
        cost_estimate=pl.CostEstimate(flops=flops, bytes_accessed=nbytes, transcendentals=0),
    )


def struct(*shape):
    return jax.ShapeDtypeStruct(shape, F32)


def times(link, field):
    out = []
    for i in range(3):
        re = im = None
        for j in range(3):
            a, b = link(0, i, j), link(1, i, j)
            x, y = field[j], field[3 + j]
            re_j, im_j = a * x - b * y, a * y + b * x
            re = re_j if re is None else re + re_j
            im = im_j if im is None else im + im_j
        out.append((re, im))
    return [o[0] for o in out] + [o[1] for o in out]


def times_dagger(link, field):
    out = []
    for i in range(3):
        re = im = None
        for j in range(3):
            a, b = link(0, j, i), link(1, j, i)
            x, y = field[j], field[3 + j]
            re_j, im_j = a * x + b * y, a * y - b * x
            re = re_j if re is None else re + re_j
            im = im_j if im is None else im + im_j
        out.append((re, im))
    return [o[0] for o in out] + [o[1] for o in out]


def lane_of(shape):
    return lax.broadcasted_iota(jnp.int32, shape, len(shape) - 1)


def z_next(x):
    axis = x.ndim - 1
    end = lane_of(x.shape) % NZ == NZ - 1
    return jnp.where(end, pltpu.roll(x, NZ - 1, axis), pltpu.roll(x, LANES - 1, axis))


def z_prev(x):
    axis = x.ndim - 1
    start = lane_of(x.shape) % NZ == 0
    return jnp.where(start, pltpu.roll(x, LANES - NZ + 1, axis), pltpu.roll(x, 1, axis))


def y_next(x):
    half = pltpu.roll(x, NZ, 1)
    return jnp.where(lane_of(x.shape) < NZ, half, pltpu.roll(half, ROWS - 1, 0))


def y_prev(x):
    half = pltpu.roll(x, NZ, 1)
    return jnp.where(lane_of(x.shape) < NZ, pltpu.roll(half, 1, 0), half)


def plane_link(g_ref, direction):
    return lambda reim, row, col: g_ref[direction * 18 + reim * 9 + row * 3 + col]


def start_body(sc, v_ref, g_ref, w_ref):
    link = plane_link(g_ref, 0)

    def one(n, carry):
        out = times_dagger(link, [v_ref[4 * k + n] for k in range(6)])
        for k in range(6):
            w_ref[pl.ds((4 * k + n) * ROWS, ROWS), :] = out[k]
        return carry

    lax.fori_loop(0, 4, one, 0)
    block = sc[0]
    for n in range(18):
        w_ref[24 * ROWS + 2 * n : 24 * ROWS + 2 * n + 2, :] = g_ref[n, pl.ds(2 * block, 2), :]
    w_ref[24 * ROWS + 36 :, :] = jnp.zeros((4, LANES), F32)


def inner_body(v_ref, g_ref, acc_ref):
    link_y, link_z = plane_link(g_ref, 1), plane_link(g_ref, 2)

    def one(n, carry):
        field = [v_ref[4 * k + n] for k in range(6)]
        total = times(link_y, [y_next(x) for x in field])
        for part in (
            [y_prev(x) for x in times_dagger(link_y, field)],
            times(link_z, [z_next(x) for x in field]),
            [z_prev(x) for x in times_dagger(link_z, field)],
        ):
            total = [a + b for a, b in zip(total, part)]
        for k in range(6):
            acc_ref[4 * k + n] = total[k]
        return carry

    lax.fori_loop(0, 4, one, 0)


def first_body(acc_ref, ahead_ref, behind_ref, g_ref, first_ref, w_ref):
    link = plane_link(g_ref, 0)

    def one(n, carry):
        hop = times(link, [ahead_ref[4 * k + n] for k in range(6)])
        first = [
            (acc_ref[4 * k + n] + hop[k] + behind_ref[pl.ds((4 * k + n) * ROWS, ROWS), :]) / -6.0
            for k in range(6)
        ]
        out = times_dagger(link, first)
        for k in range(6):
            first_ref[4 * k + n] = first[k]
            w_ref[4 * k + n] = out[k]
        return carry

    lax.fori_loop(0, 4, one, 0)


def second_body(acc_ref, ahead_ref, behind_ref, v_ref, g_ref, out_ref, f_ref, half_ref):
    link = plane_link(g_ref, 0)

    def one(n, carry):
        hop = times(link, [ahead_ref[4 * k + n] for k in range(6)])
        for k in range(6):
            r = 4 * k + n
            f = (acc_ref[r] + hop[k] + behind_ref[r]) / -3.0 - v_ref[r]
            f_ref[pl.ds(r * ROWS, ROWS), :] = f
            half_ref[pl.ds(r * ROWS, ROWS), :] = pltpu.roll(f, NZ, 1)
        return carry

    lax.fori_loop(0, 4, one, 0)
    low = lane_of((24, LANES)) < NZ
    for block in range(16):
        for q in range(2):
            out_ref[block, 24 * q : 24 * q + 24, :] = f_ref[pl.ds(2 * block + q, 24, ROWS), :]
        under = half_ref[pl.ds((2 * block - 1) % ROWS, 24, ROWS), :]
        over = half_ref[pl.ds((2 * block + 2) % ROWS, 24, ROWS), :]
        out_ref[block, 48:72, :] = jnp.where(low, under, over)


def matrix_body(sc, g_ref, behind_ref, m_ref):
    block = sc[0]
    low = lane_of((1, LANES)) < NZ
    for op in range(NDISP):
        hop = lax.rem(sc[2 + op] + 3, 6)
        direction = lax.rem(hop, 3)

        def put(reim, row, col, q, value):
            m_ref[pl.ds(((op * 18 + reim * 9 + row * 3 + col) * 2) + q, 1), :] = value

        @pl.when(hop < 3)
        def _():
            for n in range(18):
                for q in range(2):
                    m_ref[pl.ds((op * 18 + n) * 2 + q, 1), :] = g_ref[
                        direction * 18 + n, pl.ds(2 * block + q, 1), :
                    ]

        def dagger(rows_of):
            for reim in range(2):
                for row in range(3):
                    for col in range(3):
                        n = reim * 9 + col * 3 + row
                        for q in range(2):
                            value = rows_of(n, q)
                            put(reim, row, col, q, -value if reim else value)

        @pl.when(hop == 3)
        def _():
            dagger(lambda n, q: behind_ref[24 * ROWS + 2 * n + q : 24 * ROWS + 2 * n + q + 1, :])

        @pl.when(hop == 4)
        def _():
            def rows_of(n, q):
                under = g_ref[18 + n, pl.ds(lax.rem(2 * block + q + ROWS - 1, ROWS), 1), :]
                here = g_ref[18 + n, pl.ds(2 * block + q, 1), :]
                return pltpu.roll(jnp.where(low, here, under), NZ, 1)

            dagger(rows_of)

        @pl.when(hop == 5)
        def _():
            dagger(lambda n, q: z_prev(g_ref[36 + n, pl.ds(2 * block + q, 1), :]))


def rows_of_block(ref, tile, odd):
    both = ref[:, 8 * tile : 8 * tile + 8, :].reshape(8, 2, 8, LANES)
    left, right = both[:, 0], both[:, 1]
    low = lax.broadcasted_iota(jnp.int32, left.shape, 1) < 4
    if odd:
        mixed = jnp.where(low, pltpu.roll(left, 4, 1), right)
    else:
        mixed = jnp.where(low, left, pltpu.roll(right, 4, 1))
    return mixed.reshape(64, LANES)


def split(x):
    high = x.astype(jnp.bfloat16)
    return high, (x - high.astype(F32)).astype(jnp.bfloat16)


def gram_body(
    scale, sc, own_ref, other_ref, ahead_ref, behind_ref, m_ref, ph_ref, out_ref,
    f_ref, n_ref, lhs_hi, lhs_lo, rhs_hi, rhs_lo,
):
    core = sc[1]

    def column(k, q):
        return slice((2 * k + q) * LANES, (2 * k + q + 1) * LANES)

    def put_lhs(op, k, q, value):
        high, rest = split(value)
        lhs_hi[64 * op : 64 * op + 64, column(k, q)] = high
        lhs_lo[64 * op : 64 * op + 64, column(k, q)] = rest

    for q in range(2):
        for pair in range(3):
            tile = 3 * q + pair
            own = own_ref[:, 8 * tile : 8 * tile + 8, :]
            other = other_ref[:, 8 * tile : 8 * tile + 8, :]
            zero = jnp.where(core == 0, own, other)
            one = jnp.where(core == 0, other, own)
            low = lax.broadcasted_iota(jnp.int32, own.shape, 1) < 4
            even = jnp.where(low, zero, pltpu.roll(one, 4, 1)).reshape(128, LANES)
            odd = jnp.where(low, pltpu.roll(zero, 4, 1), one).reshape(128, LANES)
            for k, value in ((2 * pair, even), (2 * pair + 1, odd)):
                high, rest = split(value)
                for part, ref in ((high, rhs_hi), (rest, rhs_lo)):
                    ref[0:128, column(k, q)] = part
                    if k < 3:
                        ref[128:256, column(k + 3, q)] = -part
                    else:
                        ref[128:256, column(k - 3, q)] = part
            for odd_one in (0, 1):
                f_ref[2 * pair + odd_one, q] = rows_of_block(own_ref, tile, odd_one)
    for q in range(2):
        for op in range(NMOM):
            cosine = ph_ref[4 * op + q : 4 * op + q + 1, :]
            sine = ph_ref[4 * op + 2 + q : 4 * op + 3 + q, :]
            for c in range(3):
                re, im = f_ref[c, q], f_ref[3 + c, q]
                put_lhs(op, c, q, cosine * re + sine * im)
                put_lhs(op, 3 + c, q, cosine * im - sine * re)
    low = lane_of((64, LANES)) < NZ
    for op in range(NDISP):
        hop = lax.rem(sc[2 + op] + 3, 6)

        for which, ref in ((0, ahead_ref), (3, behind_ref)):

            @pl.when(hop == which)
            def _():
                for k in range(6):
                    for q in range(2):
                        n_ref[k, q] = rows_of_block(ref, 3 * q + k // 2, k % 2)

        @pl.when(hop == 1)
        def _():
            for k in range(6):
                edge = rows_of_block(own_ref, 6 + k // 2, k % 2)
                here, over = pltpu.roll(f_ref[k, 0], NZ, 1), pltpu.roll(f_ref[k, 1], NZ, 1)
                n_ref[k, 0] = jnp.where(low, here, over)
                n_ref[k, 1] = jnp.where(low, over, edge)

        @pl.when(hop == 4)
        def _():
            for k in range(6):
                edge = rows_of_block(own_ref, 6 + k // 2, k % 2)
                here, over = pltpu.roll(f_ref[k, 0], NZ, 1), pltpu.roll(f_ref[k, 1], NZ, 1)
                n_ref[k, 0] = jnp.where(low, edge, here)
                n_ref[k, 1] = jnp.where(low, here, over)

        @pl.when(hop == 2)
        def _():
            for k in range(6):
                for q in range(2):
                    n_ref[k, q] = z_next(f_ref[k, q])

        @pl.when(hop == 5)
        def _():
            for k in range(6):
                for q in range(2):
                    n_ref[k, q] = z_prev(f_ref[k, q])

        for q in range(2):

            def link(reim, row, col):
                at = (op * 18 + reim * 9 + row * 3 + col) * 2 + q
                return m_ref[at : at + 1, :]

            moved = times(link, [n_ref[k, q] for k in range(6)])
            for k in range(6):
                put_lhs(NMOM + op, k, q, moved[k])

    def dot(a, b):
        return lax.dot_general(
            a[...], b[...], (((1,), (1,)), ((), ())), preferred_element_type=F32
        )

    sums = dot(lhs_hi, rhs_hi) + (dot(lhs_hi, rhs_lo) + dot(lhs_lo, rhs_hi))
    tiles = [
        sums[64 * op : 64 * op + 64, 128 * reim : 128 * reim + 128] * scale
        for reim in range(2)
        for op in range(4)
    ]
    group = lane_of((64, LANES)) // 16
    for bit in (4, 2, 1):
        clear = lax.rem(group // bit, 2) == 0
        for i in range(8):
            if i & bit == 0:
                a, b = tiles[i], tiles[i + bit]
                tiles[i] = jnp.where(clear, a, pltpu.roll(b, 16 * bit, 1))
                tiles[i + bit] = jnp.where(clear, pltpu.roll(a, LANES - 16 * bit, 1), b)
    for slab in range(8):
        out_ref[slab] = tiles[slab]


def finish_body(part_ref, out_ref):
    parts = [part_ref[8 * i : 8 * i + 8, :] for i in range(64)]
    while len(parts) > 1:
        parts = [a + b for a, b in zip(parts[::2], parts[1::2])]
    total = parts[0] + pltpu.roll(parts[0], 4, 0)
    for t in range(8):
        moved = total if t == 0 else pltpu.roll(total, LANES - 16 * t, 1)
        out_ref[t] = moved[:4, :16]


def local(slabs, vecs, vectors, gauge_links, momenta, displacements):
    field_bytes = 24 * ROWS * LANES * 4
    field = vectors.reshape(24, ROWS, LANES)
    gauge = gauge_links.reshape(54, ROWS, LANES)
    slab = lax.axis_index("space")
    block = lax.axis_index("vec") // 2
    core = lax.axis_index("vec") % 2
    scalars = jnp.concatenate(
        [jnp.stack([block, core]).astype(jnp.int32), displacements.astype(jnp.int32)]
    )
    up = [(i, (i + 1) % slabs) for i in range(slabs)]
    down = [(i, (i - 1) % slabs) for i in range(slabs)]
    partner = [(i, i ^ 1) for i in range(vecs)]
    cores = [[2 * i + c for i in range(vecs // 2)] for c in range(2)]
    alike = [[2 * i + c for i in range(slabs * vecs // 2)] for c in range(2)]

    ahead = lax.ppermute(field, "space", down)
    shape = struct(24 * ROWS + 40, LANES)
    gauge_x = gauge[:18]
    w = call(start_body, shape, 2, scalars=True, flops=3 << 20, nbytes=3 * field_bytes)(
        scalars, field, gauge_x
    )
    behind = lax.ppermute(w, "space", up)
    inner = call(
        inner_body, struct(24, ROWS, LANES), 2, flops=12 << 20, nbytes=5 * field_bytes
    )
    acc = inner(field, gauge)
    first, w = call(
        first_body, [struct(24, ROWS, LANES)] * 2, 4, flops=6 << 20, nbytes=6 * field_bytes
    )(acc, ahead, behind, gauge_x)
    ahead2 = lax.ppermute(first, "space", down)
    behind2 = lax.ppermute(w, "space", up)
    acc = inner(first, gauge)
    matrices = call(
        matrix_body, struct(72, LANES), 2, scalars=True, flops=1 << 20, nbytes=4 * field_bytes
    )(scalars, gauge, behind)
    lane = jnp.arange(LANES, dtype=jnp.int32)
    row = 4 * block + 2 * jnp.arange(2, dtype=jnp.int32)[:, None] + lane[None, :] // NZ
    depth = jnp.broadcast_to(lane % NZ, row.shape)
    angles = []
    for op in range(NMOM):
        part_x = (momenta[op, 0] * slab % slabs).astype(F32) / slabs
        part_y = (momenta[op, 1] * row % NY).astype(F32) / NY
        part_z = (momenta[op, 2] * depth % NZ).astype(F32) / NZ
        angles.append((part_x + part_y + part_z) * (2.0 * math.pi))
    angle = jnp.stack(angles)
    phases = jnp.stack([jnp.cos(angle), jnp.sin(angle)], axis=1).reshape(8, LANES)
    cut = call(
        second_body,
        struct(16, 72, LANES),
        5,
        scratch=[VMEM((24 * ROWS, LANES), F32)] * 2,
        flops=6 << 20,
        nbytes=7 * field_bytes,
    )(acc, ahead2, behind2, field, gauge_x)
    own = lax.all_to_all(cut, "vec", 0, 0, axis_index_groups=cores)
    bulk = own[:, :48]
    ahead3 = lax.ppermute(bulk, "space", down)
    behind3 = lax.ppermute(bulk, "space", up)
    other = lax.ppermute(bulk, "vec", partner)
    scale = 1.0 / math.sqrt(3 * slabs * NY * NZ)
    sums = call(
        functools.partial(gram_body, scale),
        struct(slabs, 64, LANES),
        6,
        scratch=[VMEM((6, 2, 64, LANES), F32)] * 2
        + [VMEM((256, 12 * LANES), jnp.bfloat16)] * 4,
        scalars=True,
        flops=600 << 20,
        nbytes=6 * field_bytes,
    )(scalars, own, other, ahead3, behind3, matrices, phases)
    sums = sums.reshape(slabs * vecs // 2, 4, LANES)
    parts = lax.all_to_all(sums, ("space", "vec"), 0, 0, axis_index_groups=alike)
    out = call(finish_body, struct(8, 4, 16), 1)(parts.reshape(512, LANES))
    return out.reshape(2, 4, 4, 16)


def solution(mesh):
    placed = (
        P(None, None, "vec", "space", None),
        P(None, None, None, None, "space", None),
        P(),
        P(),
    )
    body = functools.partial(local, mesh.shape["space"], mesh.shape["vec"])
    return jax.shard_map(
        body, mesh=mesh, in_specs=placed, out_specs=P(None, None, "vec", "space"), check_vma=False
    )
```

```python
import functools
import math

import jax
import jax.numpy as jnp
from jax import lax
from jax.experimental import pallas as pl
from jax.experimental.pallas import tpu as pltpu
from jax.sharding import PartitionSpec as P

NY = 64
NZ = 64
NMOM = 2
NDISP = 2
ROWS = 32
LANES = 128
VMEM = pltpu.VMEM
F32 = jnp.float32


LINKS = pl.BlockSpec((18, ROWS, LANES), lambda i: (0, 0, 0))


def call(body, out_shape, ins, scratch=(), flops=0, nbytes=0, room=8):
    kinds = {
        "s": pl.BlockSpec(memory_space=pltpu.SMEM),
        "x": LINKS,
        "v": pl.BlockSpec(memory_space=VMEM),
    }
    specs = [kinds[letter] for letter in ins]
    many = isinstance(out_shape, (list, tuple))
    return pl.pallas_call(
        body,
        out_shape=out_shape,
        grid=(1,) if "x" in ins else (),
        in_specs=specs,
        out_specs=[pl.BlockSpec(memory_space=VMEM)] * len(out_shape)
        if many
        else pl.BlockSpec(memory_space=VMEM),
        scratch_shapes=list(scratch),
        cost_estimate=pl.CostEstimate(flops=flops, bytes_accessed=nbytes, transcendentals=0),
        compiler_params=pltpu.CompilerParams(vmem_limit_bytes=room << 20),
    )


def struct(*shape):
    return jax.ShapeDtypeStruct(shape, F32)


def times(link, field):
    out = []
    for i in range(3):
        re = im = None
        for j in range(3):
            a, b = link(0, i, j), link(1, i, j)
            x, y = field[j], field[3 + j]
            re_j, im_j = a * x - b * y, a * y + b * x
            re = re_j if re is None else re + re_j
            im = im_j if im is None else im + im_j
        out.append((re, im))
    return [o[0] for o in out] + [o[1] for o in out]


def times_dagger(link, field):
    out = []
    for i in range(3):
        re = im = None
        for j in range(3):
            a, b = link(0, j, i), link(1, j, i)
            x, y = field[j], field[3 + j]
            re_j, im_j = a * x + b * y, a * y - b * x
            re = re_j if re is None else re + re_j
            im = im_j if im is None else im + im_j
        out.append((re, im))
    return [o[0] for o in out] + [o[1] for o in out]


def lane_of(shape):
    return lax.broadcasted_iota(jnp.int32, shape, len(shape) - 1)


def z_next(x):
    axis = x.ndim - 1
    end = lane_of(x.shape) % NZ == NZ - 1
    return jnp.where(end, pltpu.roll(x, NZ - 1, axis), pltpu.roll(x, LANES - 1, axis))


def z_prev(x):
    axis = x.ndim - 1
    start = lane_of(x.shape) % NZ == 0
    return jnp.where(start, pltpu.roll(x, LANES - NZ + 1, axis), pltpu.roll(x, 1, axis))


def y_next(x):
    half = pltpu.roll(x, NZ, 1)
    return jnp.where(lane_of(x.shape) < NZ, half, pltpu.roll(half, ROWS - 1, 0))


def y_prev(x):
    half = pltpu.roll(x, NZ, 1)
    return jnp.where(lane_of(x.shape) < NZ, pltpu.roll(half, 1, 0), half)


def plane_link(g_ref, direction):
    return lambda reim, row, col: g_ref[direction * 18 + reim * 9 + row * 3 + col]


def start_body(v_ref, g_ref, w_ref):
    link = plane_link(g_ref, 0)

    def one(n, carry):
        out = times_dagger(link, [v_ref[4 * k + n] for k in range(6)])
        for k in range(6):
            w_ref[pl.ds((4 * k + n) * ROWS, ROWS), :] = out[k]
        return carry

    lax.fori_loop(0, 4, one, 0)
    block = lax.axis_index("vec") // 2
    for n in range(18):
        w_ref[24 * ROWS + 2 * n : 24 * ROWS + 2 * n + 2, :] = g_ref[n, pl.ds(2 * block, 2), :]
    w_ref[24 * ROWS + 36 :, :] = jnp.zeros((4, LANES), F32)


def inner_body(v_ref, g_ref, acc_ref):
    link_y, link_z = plane_link(g_ref, 1), plane_link(g_ref, 2)

    def one(n, carry):
        field = [v_ref[4 * k + n] for k in range(6)]
        total = times(link_y, [y_next(x) for x in field])
        for part in (
            [y_prev(x) for x in times_dagger(link_y, field)],
            times(link_z, [z_next(x) for x in field]),
            [z_prev(x) for x in times_dagger(link_z, field)],
        ):
            total = [a + b for a, b in zip(total, part)]
        for k in range(6):
            acc_ref[4 * k + n] = total[k]
        return carry

    lax.fori_loop(0, 4, one, 0)


def first_body(acc_ref, ahead_ref, behind_ref, g_ref, first_ref, w_ref):
    link = plane_link(g_ref, 0)

    def one(n, carry):
        hop = times(link, [ahead_ref[4 * k + n] for k in range(6)])
        first = [
            (acc_ref[4 * k + n] + hop[k] + behind_ref[pl.ds((4 * k + n) * ROWS, ROWS), :]) / -6.0
            for k in range(6)
        ]
        out = times_dagger(link, first)
        for k in range(6):
            first_ref[4 * k + n] = first[k]
            w_ref[4 * k + n] = out[k]
        return carry

    lax.fori_loop(0, 4, one, 0)


def second_body(acc_ref, ahead_ref, behind_ref, v_ref, g_ref, out_ref, f_ref, half_ref):
    link = plane_link(g_ref, 0)

    def one(n, carry):
        hop = times(link, [ahead_ref[4 * k + n] for k in range(6)])
        for k in range(6):
            r = 4 * k + n
            f = (acc_ref[r] + hop[k] + behind_ref[r]) / -3.0 - v_ref[r]
            f_ref[pl.ds(r * ROWS, ROWS), :] = f
            half_ref[pl.ds(r * ROWS, ROWS), :] = pltpu.roll(f, NZ, 1)
        return carry

    lax.fori_loop(0, 4, one, 0)
    low = lane_of((24, LANES)) < NZ
    for block in range(16):
        for q in range(2):
            out_ref[block, 24 * q : 24 * q + 24, :] = f_ref[pl.ds(2 * block + q, 24, ROWS), :]
        under = half_ref[pl.ds((2 * block - 1) % ROWS, 24, ROWS), :]
        over = half_ref[pl.ds((2 * block + 2) % ROWS, 24, ROWS), :]
        out_ref[block, 48:72, :] = jnp.where(low, under, over)


def matrix_body(sc, g_ref, behind_ref, m_ref):
    block = lax.axis_index("vec") // 2
    low = lane_of((1, LANES)) < NZ
    for op in range(NDISP):
        hop = lax.rem(sc[op] + 3, 6)
        direction = lax.rem(hop, 3)

        def put(reim, row, col, q, value):
            m_ref[pl.ds(((op * 18 + reim * 9 + row * 3 + col) * 2) + q, 1), :] = value

        @pl.when(hop < 3)
        def _():
            for n in range(18):
                for q in range(2):
                    m_ref[pl.ds((op * 18 + n) * 2 + q, 1), :] = g_ref[
                        direction * 18 + n, pl.ds(2 * block + q, 1), :
                    ]

        def dagger(rows_of):
            for reim in range(2):
                for row in range(3):
                    for col in range(3):
                        n = reim * 9 + col * 3 + row
                        for q in range(2):
                            value = rows_of(n, q)
                            put(reim, row, col, q, -value if reim else value)

        @pl.when(hop == 3)
        def _():
            dagger(lambda n, q: behind_ref[24 * ROWS + 2 * n + q : 24 * ROWS + 2 * n + q + 1, :])

        @pl.when(hop == 4)
        def _():
            def rows_of(n, q):
                under = g_ref[18 + n, pl.ds(lax.rem(2 * block + q + ROWS - 1, ROWS), 1), :]
                here = g_ref[18 + n, pl.ds(2 * block + q, 1), :]
                return pltpu.roll(jnp.where(low, here, under), NZ, 1)

            dagger(rows_of)

        @pl.when(hop == 5)
        def _():
            dagger(lambda n, q: z_prev(g_ref[36 + n, pl.ds(2 * block + q, 1), :]))


def rows_of_block(ref, tile, odd):
    both = ref[:, 8 * tile : 8 * tile + 8, :].reshape(8, 2, 8, LANES)
    left, right = both[:, 0], both[:, 1]
    low = lax.broadcasted_iota(jnp.int32, left.shape, 1) < 4
    if odd:
        mixed = jnp.where(low, pltpu.roll(left, 4, 1), right)
    else:
        mixed = jnp.where(low, left, pltpu.roll(right, 4, 1))
    return mixed.reshape(64, LANES)


def split(x):
    high = x.astype(jnp.bfloat16)
    return high, (x - high.astype(F32)).astype(jnp.bfloat16)


def gram_body(
    scale, sc, own_ref, other_ref, ahead_ref, behind_ref, m_ref, ph_ref, out_ref,
    f_ref, n_ref, lhs_hi, lhs_lo, rhs_hi, rhs_lo,
):
    core = lax.rem(lax.axis_index("vec"), 2)

    def column(k, q):
        return slice((2 * k + q) * LANES, (2 * k + q + 1) * LANES)

    def put_lhs(op, k, q, value):
        high, rest = split(value)
        lhs_hi[64 * op : 64 * op + 64, column(k, q)] = high
        lhs_lo[64 * op : 64 * op + 64, column(k, q)] = rest

    for q in range(2):
        for pair in range(3):
            tile = 3 * q + pair
            own = own_ref[:, 8 * tile : 8 * tile + 8, :]
            other = other_ref[:, 8 * tile : 8 * tile + 8, :]
            zero = jnp.where(core == 0, own, other)
            one = jnp.where(core == 0, other, own)
            low = lax.broadcasted_iota(jnp.int32, own.shape, 1) < 4
            even = jnp.where(low, zero, pltpu.roll(one, 4, 1)).reshape(128, LANES)
            odd = jnp.where(low, pltpu.roll(zero, 4, 1), one).reshape(128, LANES)
            for k, value in ((2 * pair, even), (2 * pair + 1, odd)):
                high, rest = split(value)
                for part, ref in ((high, rhs_hi), (rest, rhs_lo)):
                    ref[0:128, column(k, q)] = part
                    if k < 3:
                        ref[128:256, column(k + 3, q)] = -part
                    else:
                        ref[128:256, column(k - 3, q)] = part
            for odd_one in (0, 1):
                f_ref[2 * pair + odd_one, q] = rows_of_block(own_ref, tile, odd_one)
    for q in range(2):
        for op in range(NMOM):
            cosine = ph_ref[4 * op + q : 4 * op + q + 1, :]
            sine = ph_ref[4 * op + 2 + q : 4 * op + 3 + q, :]
            for c in range(3):
                re, im = f_ref[c, q], f_ref[3 + c, q]
                put_lhs(op, c, q, cosine * re + sine * im)
                put_lhs(op, 3 + c, q, cosine * im - sine * re)
    low = lane_of((64, LANES)) < NZ
    for op in range(NDISP):
        hop = lax.rem(sc[op] + 3, 6)

        for which, ref in ((0, ahead_ref), (3, behind_ref)):

            @pl.when(hop == which)
            def _():
                for k in range(6):
                    for q in range(2):
                        n_ref[k, q] = rows_of_block(ref, 3 * q + k // 2, k % 2)

        @pl.when(hop == 1)
        def _():
            for k in range(6):
                edge = rows_of_block(own_ref, 6 + k // 2, k % 2)
                here, over = pltpu.roll(f_ref[k, 0], NZ, 1), pltpu.roll(f_ref[k, 1], NZ, 1)
                n_ref[k, 0] = jnp.where(low, here, over)
                n_ref[k, 1] = jnp.where(low, over, edge)

        @pl.when(hop == 4)
        def _():
            for k in range(6):
                edge = rows_of_block(own_ref, 6 + k // 2, k % 2)
                here, over = pltpu.roll(f_ref[k, 0], NZ, 1), pltpu.roll(f_ref[k, 1], NZ, 1)
                n_ref[k, 0] = jnp.where(low, edge, here)
                n_ref[k, 1] = jnp.where(low, here, over)

        @pl.when(hop == 2)
        def _():
            for k in range(6):
                for q in range(2):
                    n_ref[k, q] = z_next(f_ref[k, q])

        @pl.when(hop == 5)
        def _():
            for k in range(6):
                for q in range(2):
                    n_ref[k, q] = z_prev(f_ref[k, q])

        for q in range(2):

            def link(reim, row, col):
                at = (op * 18 + reim * 9 + row * 3 + col) * 2 + q
                return m_ref[at : at + 1, :]

            moved = times(link, [n_ref[k, q] for k in range(6)])
            for k in range(6):
                put_lhs(NMOM + op, k, q, moved[k])

    def dot(a, b):
        return lax.dot_general(
            a[...], b[...], (((1,), (1,)), ((), ())), preferred_element_type=F32
        )

    sums = dot(lhs_hi, rhs_hi) + (dot(lhs_hi, rhs_lo) + dot(lhs_lo, rhs_hi))
    tiles = [
        sums[64 * op : 64 * op + 64, 128 * reim : 128 * reim + 128] * scale
        for reim in range(2)
        for op in range(4)
    ]
    group = lane_of((64, LANES)) // 16
    for bit in (4, 2, 1):
        clear = lax.rem(group // bit, 2) == 0
        for i in range(8):
            if i & bit == 0:
                a, b = tiles[i], tiles[i + bit]
                tiles[i] = jnp.where(clear, a, pltpu.roll(b, 16 * bit, 1))
                tiles[i + bit] = jnp.where(clear, pltpu.roll(a, LANES - 16 * bit, 1), b)
    for slab in range(8):
        out_ref[slab] = tiles[slab]


def finish_body(part_ref, out_ref):
    parts = [part_ref[8 * i : 8 * i + 8, :] for i in range(64)]
    while len(parts) > 1:
        parts = [a + b for a, b in zip(parts[::2], parts[1::2])]
    total = parts[0] + pltpu.roll(parts[0], 4, 0)
    for t in range(8):
        moved = total if t == 0 else pltpu.roll(total, LANES - 16 * t, 1)
        out_ref[t] = moved[:4, :16]


def local(slabs, vecs, vectors, gauge_links, momenta, displacements):
    field_bytes = 24 * ROWS * LANES * 4
    field = vectors.reshape(24, ROWS, LANES)
    gauge = gauge_links.reshape(54, ROWS, LANES)
    slab = lax.axis_index("space")
    block = lax.axis_index("vec") // 2
    up = [(i, (i + 1) % slabs) for i in range(slabs)]
    down = [(i, (i - 1) % slabs) for i in range(slabs)]
    partner = [(i, i ^ 1) for i in range(vecs)]
    cores = [[2 * i + c for i in range(vecs // 2)] for c in range(2)]
    alike = [[2 * i + c for i in range(slabs * vecs // 2)] for c in range(2)]

    ahead = lax.ppermute(field, "space", down)
    shape = struct(24 * ROWS + 40, LANES)
    w = call(start_body, shape, "vx", flops=3 << 20, nbytes=3 * field_bytes)(field, gauge)
    behind = lax.ppermute(w, "space", up)
    inner = call(
        inner_body, struct(24, ROWS, LANES), "vv", flops=12 << 20, nbytes=5 * field_bytes
    )
    acc = inner(field, gauge)
    first, w = call(
        first_body, [struct(24, ROWS, LANES)] * 2, "vvvx", flops=6 << 20, nbytes=6 * field_bytes
    )(acc, ahead, behind, gauge)
    ahead2 = lax.ppermute(first, "space", down)
    behind2 = lax.ppermute(w, "space", up)
    acc = inner(first, gauge)
    matrices = call(
        matrix_body, struct(72, LANES), "svv", flops=1 << 20, nbytes=4 * field_bytes
    )(displacements, gauge, behind)
    lane = jnp.arange(LANES, dtype=jnp.int32)
    row = 4 * block + 2 * jnp.arange(2, dtype=jnp.int32)[:, None] + lane[None, :] // NZ
    depth = jnp.broadcast_to(lane % NZ, row.shape)
    angles = []
    for op in range(NMOM):
        part_x = (momenta[op, 0] * slab % slabs).astype(F32) / slabs
        part_y = (momenta[op, 1] * row % NY).astype(F32) / NY
        part_z = (momenta[op, 2] * depth % NZ).astype(F32) / NZ
        angles.append((part_x + part_y + part_z) * (2.0 * math.pi))
    angle = jnp.stack(angles)
    phases = jnp.stack([jnp.cos(angle), jnp.sin(angle)], axis=1).reshape(8, LANES)
    cut = call(
        second_body,
        struct(16, 72, LANES),
        "vvvvx",
        scratch=[VMEM((24 * ROWS, LANES), F32)] * 2,
        flops=6 << 20,
        nbytes=7 * field_bytes,
    )(acc, ahead2, behind2, field, gauge)
    own = lax.all_to_all(cut, "vec", 0, 0, axis_index_groups=cores)
    bulk = own[:, :48]
    ahead3 = lax.ppermute(bulk, "space", down)
    behind3 = lax.ppermute(bulk, "space", up)
    other = lax.ppermute(bulk, "vec", partner)
    scale = 1.0 / math.sqrt(3 * slabs * NY * NZ)
    sums = call(
        functools.partial(gram_body, scale),
        struct(slabs, 64, LANES),
        "svvvvvv",
        scratch=[VMEM((6, 2, 64, LANES), F32)] * 2
        + [VMEM((256, 12 * LANES), jnp.bfloat16)] * 4,
        room=16,
        flops=600 << 20,
        nbytes=6 * field_bytes,
    )(displacements, own, other, ahead3, behind3, matrices, phases)
    sums = sums.reshape(slabs * vecs // 2, 4, LANES)
    parts = lax.all_to_all(sums, ("space", "vec"), 0, 0, axis_index_groups=alike)
    out = call(finish_body, struct(8, 4, 16), "v")(parts.reshape(512, LANES))
    return out.reshape(2, 4, 4, 16)


def solution(mesh):
    placed = (
        P(None, None, "vec", "space", None),
        P(None, None, None, None, "space", None),
        P(),
        P(),
    )
    body = functools.partial(local, mesh.shape["space"], mesh.shape["vec"])
    return jax.shard_map(
        body, mesh=mesh, in_specs=placed, out_specs=P(None, None, "vec", "space"), check_vma=False
    )
```

```python
import functools
import math

import jax
import jax.numpy as jnp
from jax import lax
from jax.experimental import pallas as pl
from jax.experimental.pallas import tpu as pltpu
from jax.sharding import PartitionSpec as P

NY = 64
NZ = 64
NMOM = 2
NDISP = 2
ROWS = 32
LANES = 128
VMEM = pltpu.VMEM
F32 = jnp.float32


LINKS = pl.BlockSpec((18, ROWS, LANES), lambda i: (0, 0, 0))


def call(body, out_shape, ins, scratch=(), flops=0, nbytes=0, room=8):
    kinds = {
        "s": pl.BlockSpec(memory_space=pltpu.SMEM),
        "x": LINKS,
        "v": pl.BlockSpec(memory_space=VMEM),
    }
    specs = [kinds[letter] for letter in ins]
    many = isinstance(out_shape, (list, tuple))
    return pl.pallas_call(
        body,
        out_shape=out_shape,
        grid=(1,) if "x" in ins else (),
        in_specs=specs,
        out_specs=[pl.BlockSpec(memory_space=VMEM)] * len(out_shape)
        if many
        else pl.BlockSpec(memory_space=VMEM),
        scratch_shapes=list(scratch),
        cost_estimate=pl.CostEstimate(flops=flops, bytes_accessed=nbytes, transcendentals=0),
        compiler_params=pltpu.CompilerParams(vmem_limit_bytes=room << 20),
    )


def struct(*shape):
    return jax.ShapeDtypeStruct(shape, F32)


def times(link, field):
    out = []
    for i in range(3):
        re = im = None
        for j in range(3):
            a, b = link(0, i, j), link(1, i, j)
            x, y = field[j], field[3 + j]
            re_j, im_j = a * x - b * y, a * y + b * x
            re = re_j if re is None else re + re_j
            im = im_j if im is None else im + im_j
        out.append((re, im))
    return [o[0] for o in out] + [o[1] for o in out]


def times_dagger(link, field):
    out = []
    for i in range(3):
        re = im = None
        for j in range(3):
            a, b = link(0, j, i), link(1, j, i)
            x, y = field[j], field[3 + j]
            re_j, im_j = a * x + b * y, a * y - b * x
            re = re_j if re is None else re + re_j
            im = im_j if im is None else im + im_j
        out.append((re, im))
    return [o[0] for o in out] + [o[1] for o in out]


def lane_of(shape):
    return lax.broadcasted_iota(jnp.int32, shape, len(shape) - 1)


def z_next(x):
    axis = x.ndim - 1
    end = lane_of(x.shape) % NZ == NZ - 1
    return jnp.where(end, pltpu.roll(x, NZ - 1, axis), pltpu.roll(x, LANES - 1, axis))


def z_prev(x):
    axis = x.ndim - 1
    start = lane_of(x.shape) % NZ == 0
    return jnp.where(start, pltpu.roll(x, LANES - NZ + 1, axis), pltpu.roll(x, 1, axis))


def y_next(x):
    half = pltpu.roll(x, NZ, 1)
    return jnp.where(lane_of(x.shape) < NZ, half, pltpu.roll(half, ROWS - 1, 0))


def y_prev(x):
    half = pltpu.roll(x, NZ, 1)
    return jnp.where(lane_of(x.shape) < NZ, pltpu.roll(half, 1, 0), half)


def plane_link(g_ref, direction):
    return lambda reim, row, col: g_ref[direction * 18 + reim * 9 + row * 3 + col]


def start_body(v_ref, g_ref, w_ref):
    link = plane_link(g_ref, 0)

    def one(n, carry):
        out = times_dagger(link, [v_ref[4 * k + n] for k in range(6)])
        for k in range(6):
            w_ref[pl.ds((4 * k + n) * ROWS, ROWS), :] = out[k]
        return carry

    lax.fori_loop(0, 4, one, 0)
    block = lax.axis_index("vec") // 2
    for n in range(18):
        w_ref[24 * ROWS + 2 * n : 24 * ROWS + 2 * n + 2, :] = g_ref[n, pl.ds(2 * block, 2), :]
    w_ref[24 * ROWS + 36 :, :] = jnp.zeros((4, LANES), F32)


def inner_body(v_ref, g_ref, acc_ref):
    link_y, link_z = plane_link(g_ref, 1), plane_link(g_ref, 2)

    def one(n, carry):
        field = [v_ref[4 * k + n] for k in range(6)]
        total = times(link_y, [y_next(x) for x in field])
        for part in (
            [y_prev(x) for x in times_dagger(link_y, field)],
            times(link_z, [z_next(x) for x in field]),
            [z_prev(x) for x in times_dagger(link_z, field)],
        ):
            total = [a + b for a, b in zip(total, part)]
        for k in range(6):
            acc_ref[4 * k + n] = total[k]
        return carry

    lax.fori_loop(0, 4, one, 0)


def first_body(acc_ref, ahead_ref, behind_ref, g_ref, first_ref, w_ref):
    link = plane_link(g_ref, 0)

    def one(n, carry):
        hop = times(link, [ahead_ref[4 * k + n] for k in range(6)])
        first = [
            (acc_ref[4 * k + n] + hop[k] + behind_ref[pl.ds((4 * k + n) * ROWS, ROWS), :]) / -6.0
            for k in range(6)
        ]
        out = times_dagger(link, first)
        for k in range(6):
            first_ref[4 * k + n] = first[k]
            w_ref[4 * k + n] = out[k]
        return carry

    lax.fori_loop(0, 4, one, 0)


def second_body(edges, acc_ref, ahead_ref, behind_ref, v_ref, g_ref, out_ref, f_ref, half_ref):
    link = plane_link(g_ref, 0)

    def one(n, carry):
        hop = times(link, [ahead_ref[4 * k + n] for k in range(6)])
        for k in range(6):
            r = 4 * k + n
            f = (acc_ref[r] + hop[k] + behind_ref[r]) / -3.0 - v_ref[r]
            f_ref[pl.ds(r * ROWS, ROWS), :] = f
            if edges:
                half_ref[pl.ds(r * ROWS, ROWS), :] = pltpu.roll(f, NZ, 1)
        return carry

    lax.fori_loop(0, 4, one, 0)
    low = lane_of((24, LANES)) < NZ
    for block in range(16):
        for q in range(2):
            out_ref[block, 24 * q : 24 * q + 24, :] = f_ref[pl.ds(2 * block + q, 24, ROWS), :]
        if not edges:
            continue
        under = half_ref[pl.ds((2 * block - 1) % ROWS, 24, ROWS), :]
        over = half_ref[pl.ds((2 * block + 2) % ROWS, 24, ROWS), :]
        out_ref[block, 48:72, :] = jnp.where(low, under, over)


def matrix_body(sc, g_ref, behind_ref, m_ref):
    block = lax.axis_index("vec") // 2
    low = lane_of((1, LANES)) < NZ
    for op in range(NDISP):
        hop = lax.rem(sc[op] + 3, 6)
        direction = lax.rem(hop, 3)

        def put(reim, row, col, q, value):
            m_ref[pl.ds(((op * 18 + reim * 9 + row * 3 + col) * 2) + q, 1), :] = value

        @pl.when(hop < 3)
        def _():
            for n in range(18):
                for q in range(2):
                    m_ref[pl.ds((op * 18 + n) * 2 + q, 1), :] = g_ref[
                        direction * 18 + n, pl.ds(2 * block + q, 1), :
                    ]

        def dagger(rows_of):
            for reim in range(2):
                for row in range(3):
                    for col in range(3):
                        n = reim * 9 + col * 3 + row
                        for q in range(2):
                            value = rows_of(n, q)
                            put(reim, row, col, q, -value if reim else value)

        @pl.when(hop == 3)
        def _():
            dagger(lambda n, q: behind_ref[24 * ROWS + 2 * n + q : 24 * ROWS + 2 * n + q + 1, :])

        @pl.when(hop == 4)
        def _():
            def rows_of(n, q):
                under = g_ref[18 + n, pl.ds(lax.rem(2 * block + q + ROWS - 1, ROWS), 1), :]
                here = g_ref[18 + n, pl.ds(2 * block + q, 1), :]
                return pltpu.roll(jnp.where(low, here, under), NZ, 1)

            dagger(rows_of)

        @pl.when(hop == 5)
        def _():
            dagger(lambda n, q: z_prev(g_ref[36 + n, pl.ds(2 * block + q, 1), :]))


def rows_of_block(ref, tile, odd):
    both = ref[:, 8 * tile : 8 * tile + 8, :].reshape(8, 2, 8, LANES)
    left, right = both[:, 0], both[:, 1]
    low = lax.broadcasted_iota(jnp.int32, left.shape, 1) < 4
    if odd:
        mixed = jnp.where(low, pltpu.roll(left, 4, 1), right)
    else:
        mixed = jnp.where(low, left, pltpu.roll(right, 4, 1))
    return mixed.reshape(64, LANES)


def split(x):
    high = x.astype(jnp.bfloat16)
    return high, (x - high.astype(F32)).astype(jnp.bfloat16)


def gram_body(
    scale, along_x, along_y, sc, own_ref, other_ref, ahead_ref, behind_ref, m_ref, ph_ref, out_ref,
    f_ref, n_ref, lhs_hi, lhs_lo, rhs_hi, rhs_lo,
):
    core = lax.rem(lax.axis_index("vec"), 2)

    def column(k, q):
        return slice((2 * k + q) * LANES, (2 * k + q + 1) * LANES)

    def put_lhs(op, k, q, value):
        high, rest = split(value)
        lhs_hi[64 * op : 64 * op + 64, column(k, q)] = high
        lhs_lo[64 * op : 64 * op + 64, column(k, q)] = rest

    for q in range(2):
        for pair in range(3):
            tile = 3 * q + pair
            own = own_ref[:, 8 * tile : 8 * tile + 8, :]
            other = other_ref[:, 8 * tile : 8 * tile + 8, :]
            zero = jnp.where(core == 0, own, other)
            one = jnp.where(core == 0, other, own)
            low = lax.broadcasted_iota(jnp.int32, own.shape, 1) < 4
            even = jnp.where(low, zero, pltpu.roll(one, 4, 1)).reshape(128, LANES)
            odd = jnp.where(low, pltpu.roll(zero, 4, 1), one).reshape(128, LANES)
            for k, value in ((2 * pair, even), (2 * pair + 1, odd)):
                high, rest = split(value)
                for part, ref in ((high, rhs_hi), (rest, rhs_lo)):
                    ref[0:128, column(k, q)] = part
                    if k < 3:
                        ref[128:256, column(k + 3, q)] = -part
                    else:
                        ref[128:256, column(k - 3, q)] = part
            for odd_one in (0, 1):
                f_ref[2 * pair + odd_one, q] = rows_of_block(own_ref, tile, odd_one)
    for q in range(2):
        for op in range(NMOM):
            cosine = ph_ref[4 * op + q : 4 * op + q + 1, :]
            sine = ph_ref[4 * op + 2 + q : 4 * op + 3 + q, :]
            for c in range(3):
                re, im = f_ref[c, q], f_ref[3 + c, q]
                put_lhs(op, c, q, cosine * re + sine * im)
                put_lhs(op, 3 + c, q, cosine * im - sine * re)
    low = lane_of((64, LANES)) < NZ
    for op in range(NDISP):
        hop = lax.rem(sc[op] + 3, 6)

        for which, ref in ((0, ahead_ref), (3, behind_ref)) if along_x else ():

            @pl.when(hop == which)
            def _():
                for k in range(6):
                    for q in range(2):
                        n_ref[k, q] = rows_of_block(ref, 3 * q + k // 2, k % 2)

        def y_ahead():
            for k in range(6):
                edge = rows_of_block(own_ref, 6 + k // 2, k % 2)
                here, over = pltpu.roll(f_ref[k, 0], NZ, 1), pltpu.roll(f_ref[k, 1], NZ, 1)
                n_ref[k, 0] = jnp.where(low, here, over)
                n_ref[k, 1] = jnp.where(low, over, edge)

        def y_behind():
            for k in range(6):
                edge = rows_of_block(own_ref, 6 + k // 2, k % 2)
                here, over = pltpu.roll(f_ref[k, 0], NZ, 1), pltpu.roll(f_ref[k, 1], NZ, 1)
                n_ref[k, 0] = jnp.where(low, edge, here)
                n_ref[k, 1] = jnp.where(low, here, over)

        if along_y:
            pl.when(hop == 1)(y_ahead)
            pl.when(hop == 4)(y_behind)

        @pl.when(hop == 2)
        def _():
            for k in range(6):
                for q in range(2):
                    n_ref[k, q] = z_next(f_ref[k, q])

        @pl.when(hop == 5)
        def _():
            for k in range(6):
                for q in range(2):
                    n_ref[k, q] = z_prev(f_ref[k, q])

        for q in range(2):

            def link(reim, row, col):
                at = (op * 18 + reim * 9 + row * 3 + col) * 2 + q
                return m_ref[at : at + 1, :]

            moved = times(link, [n_ref[k, q] for k in range(6)])
            for k in range(6):
                put_lhs(NMOM + op, k, q, moved[k])

    def dot(a, b):
        return lax.dot_general(
            a[...], b[...], (((1,), (1,)), ((), ())), preferred_element_type=F32
        )

    sums = dot(lhs_hi, rhs_hi) + (dot(lhs_hi, rhs_lo) + dot(lhs_lo, rhs_hi))
    tiles = [
        sums[64 * op : 64 * op + 64, 128 * reim : 128 * reim + 128] * scale
        for reim in range(2)
        for op in range(4)
    ]
    group = lane_of((64, LANES)) // 16
    for bit in (4, 2, 1):
        clear = lax.rem(group // bit, 2) == 0
        for i in range(8):
            if i & bit == 0:
                a, b = tiles[i], tiles[i + bit]
                tiles[i] = jnp.where(clear, a, pltpu.roll(b, 16 * bit, 1))
                tiles[i + bit] = jnp.where(clear, pltpu.roll(a, LANES - 16 * bit, 1), b)
    for slab in range(8):
        out_ref[slab] = tiles[slab]


def finish_body(part_ref, out_ref):
    parts = [part_ref[8 * i : 8 * i + 8, :] for i in range(64)]
    while len(parts) > 1:
        parts = [a + b for a, b in zip(parts[::2], parts[1::2])]
    total = parts[0] + pltpu.roll(parts[0], 4, 0)
    for t in range(8):
        moved = total if t == 0 else pltpu.roll(total, LANES - 16 * t, 1)
        out_ref[t] = moved[:4, :16]


def local(slabs, vecs, vectors, gauge_links, momenta, displacements):
    field_bytes = 24 * ROWS * LANES * 4
    field = vectors.reshape(24, ROWS, LANES)
    gauge = gauge_links.reshape(54, ROWS, LANES)
    slab = lax.axis_index("space")
    block = lax.axis_index("vec") // 2
    up = [(i, (i + 1) % slabs) for i in range(slabs)]
    down = [(i, (i - 1) % slabs) for i in range(slabs)]
    partner = [(i, i ^ 1) for i in range(vecs)]
    cores = [[2 * i + c for i in range(vecs // 2)] for c in range(2)]
    alike = [[2 * i + c for i in range(slabs * vecs // 2)] for c in range(2)]

    shape = struct(24 * ROWS + 40, LANES)
    w = call(start_body, shape, "vx", flops=3 << 20, nbytes=3 * field_bytes)(field, gauge)
    first_out, w = lax.optimization_barrier((field, w))
    behind = lax.ppermute(w, "space", up)
    ahead = lax.ppermute(first_out, "space", down)
    inner = call(
        inner_body, struct(24, ROWS, LANES), "vv", flops=12 << 20, nbytes=5 * field_bytes
    )
    acc = inner(field, gauge)
    first, w = call(
        first_body, [struct(24, ROWS, LANES)] * 2, "vvvx", flops=6 << 20, nbytes=6 * field_bytes
    )(acc, ahead, behind, gauge)
    ahead2 = lax.ppermute(first, "space", down)
    behind2 = lax.ppermute(w, "space", up)
    acc = inner(first, gauge)
    matrices = call(
        matrix_body, struct(72, LANES), "svv", flops=1 << 20, nbytes=4 * field_bytes
    )(displacements, gauge, behind)
    lane = jnp.arange(LANES, dtype=jnp.int32)
    row = 4 * block + 2 * jnp.arange(2, dtype=jnp.int32)[:, None] + lane[None, :] // NZ
    depth = jnp.broadcast_to(lane % NZ, row.shape)
    angles = []
    for op in range(NMOM):
        part_x = (momenta[op, 0] * slab % slabs).astype(F32) / slabs
        part_y = (momenta[op, 1] * row % NY).astype(F32) / NY
        part_z = (momenta[op, 2] * depth % NZ).astype(F32) / NZ
        angles.append((part_x + part_y + part_z) * (2.0 * math.pi))
    angle = jnp.stack(angles)
    phases = jnp.stack([jnp.cos(angle), jnp.sin(angle)], axis=1).reshape(8, LANES)
    along = displacements % 3
    case = jnp.any(along == 0).astype(jnp.int32) + 2 * jnp.any(along == 1).astype(jnp.int32)
    acc, phases, matrices, case = lax.optimization_barrier((acc, phases, matrices, case))
    scale = 1.0 / math.sqrt(3 * slabs * NY * NZ)

    def elementals(along_x, along_y, acc, ahead2, behind2, field, gauge, phases, matrices):
        cut = call(
            functools.partial(second_body, along_y),
            struct(16, 72 if along_y else 48, LANES),
            "vvvvx",
            scratch=[VMEM((24 * ROWS, LANES), F32)] * 2,
            flops=6 << 20,
            nbytes=7 * field_bytes,
        )(acc, ahead2, behind2, field, gauge)
        own = lax.all_to_all(cut, "vec", 0, 0, axis_index_groups=cores)
        bulk = own[:, :48]
        ahead3 = behind3 = bulk
        if along_x:
            ahead3 = lax.ppermute(bulk, "space", down)
            behind3 = lax.ppermute(bulk, "space", up)
        other = lax.ppermute(bulk, "vec", partner)
        sums = call(
            functools.partial(gram_body, scale, along_x, along_y),
            struct(slabs, 64, LANES),
            "svvvvvv",
            scratch=[VMEM((6, 2, 64, LANES), F32)] * 2
            + [VMEM((256, 12 * LANES), jnp.bfloat16)] * 4,
            room=16,
            flops=600 << 20,
            nbytes=6 * field_bytes,
        )(displacements, own, other, ahead3, behind3, matrices, phases)
        sums = sums.reshape(slabs * vecs // 2, 4, LANES)
        parts = lax.all_to_all(sums, ("space", "vec"), 0, 0, axis_index_groups=alike)
        return call(finish_body, struct(8, 4, 16), "v")(parts.reshape(512, LANES))

    out = lax.switch(
        case,
        [
            functools.partial(elementals, bool(i & 1), bool(i & 2))
            for i in range(4)
        ],
        acc, ahead2, behind2, field, gauge, phases, matrices,
    )
    return out.reshape(2, 4, 4, 16)


def solution(mesh):
    placed = (
        P(None, None, "vec", "space", None),
        P(None, None, None, None, "space", None),
        P(),
        P(),
    )
    body = functools.partial(local, mesh.shape["space"], mesh.shape["vec"])
    return jax.shard_map(
        body, mesh=mesh, in_specs=placed, out_specs=P(None, None, "vec", "space"), check_vma=False
    )
```

```python
import functools
import math

import jax
import jax.numpy as jnp
from jax import lax
from jax.experimental import pallas as pl
from jax.experimental.pallas import tpu as pltpu
from jax.sharding import PartitionSpec as P

NY = 64
NZ = 64
NMOM = 2
NDISP = 2
ROWS = 32
LANES = 128
PHASES = 36 * NDISP
VMEM = pltpu.VMEM
F32 = jnp.float32


LINKS = pl.BlockSpec((18, ROWS, LANES), lambda i: (0, 0, 0))


SMEM_BLOCK = pl.BlockSpec(memory_space=pltpu.SMEM)


def call(body, out_shape, ins, scratch=(), flops=0, nbytes=0, room=8):
    kinds = {
        "s": SMEM_BLOCK,
        "x": LINKS,
        "v": pl.BlockSpec(memory_space=VMEM),
        "h": pl.BlockSpec(memory_space=pl.ANY),
    }
    specs = [kinds[letter] for letter in ins]
    many = isinstance(out_shape, (list, tuple))
    return pl.pallas_call(
        body,
        out_shape=out_shape,
        grid=(1,) if "x" in ins else (),
        in_specs=specs,
        out_specs=[
            pl.BlockSpec(memory_space=VMEM) if each.dtype != jnp.int32 else SMEM_BLOCK
            for each in out_shape
        ]
        if many
        else pl.BlockSpec(memory_space=VMEM),
        scratch_shapes=list(scratch),
        cost_estimate=pl.CostEstimate(flops=flops, bytes_accessed=nbytes, transcendentals=0),
        compiler_params=pltpu.CompilerParams(vmem_limit_bytes=room << 20),
    )


def struct(*shape):
    return jax.ShapeDtypeStruct(shape, F32)


def times(link, field):
    out = []
    for i in range(3):
        re = im = None
        for j in range(3):
            a, b = link(0, i, j), link(1, i, j)
            x, y = field[j], field[3 + j]
            re_j, im_j = a * x - b * y, a * y + b * x
            re = re_j if re is None else re + re_j
            im = im_j if im is None else im + im_j
        out.append((re, im))
    return [o[0] for o in out] + [o[1] for o in out]


def times_dagger(link, field):
    out = []
    for i in range(3):
        re = im = None
        for j in range(3):
            a, b = link(0, j, i), link(1, j, i)
            x, y = field[j], field[3 + j]
            re_j, im_j = a * x + b * y, a * y - b * x
            re = re_j if re is None else re + re_j
            im = im_j if im is None else im + im_j
        out.append((re, im))
    return [o[0] for o in out] + [o[1] for o in out]


def lane_of(shape):
    return lax.broadcasted_iota(jnp.int32, shape, len(shape) - 1)


def z_next(x):
    axis = x.ndim - 1
    end = lane_of(x.shape) % NZ == NZ - 1
    return jnp.where(end, pltpu.roll(x, NZ - 1, axis), pltpu.roll(x, LANES - 1, axis))


def z_prev(x):
    axis = x.ndim - 1
    start = lane_of(x.shape) % NZ == 0
    return jnp.where(start, pltpu.roll(x, LANES - NZ + 1, axis), pltpu.roll(x, 1, axis))


def y_next(x):
    half = pltpu.roll(x, NZ, 1)
    return jnp.where(lane_of(x.shape) < NZ, half, pltpu.roll(half, ROWS - 1, 0))


def y_prev(x):
    half = pltpu.roll(x, NZ, 1)
    return jnp.where(lane_of(x.shape) < NZ, pltpu.roll(half, 1, 0), half)


def plane_link(g_ref, direction):
    return lambda reim, row, col: g_ref[direction * 18 + reim * 9 + row * 3 + col]


def start_body(v_hbm, g_hbm, va_ref, vb_ref, wa_ref, wb_ref, g_ref, sems):
    copies = []
    for i in range(6):
        for half, v_ref in enumerate((va_ref, vb_ref)):
            copies.append(
                pltpu.make_async_copy(
                    v_hbm.at[pl.ds(4 * i + 2 * half, 2)],
                    v_ref.at[pl.ds(2 * i, 2)],
                    sems.at[2 * i + half],
                )
            )
        copies.append(
            pltpu.make_async_copy(
                g_hbm.at[pl.ds(3 * i, 3)], g_ref.at[pl.ds(3 * i, 3)], sems.at[12 + i]
            )
        )
    for copy in copies:
        copy.start()
    for copy in copies:
        copy.wait()
    link = plane_link(g_ref, 0)
    for v_ref, w_ref in ((va_ref, wa_ref), (vb_ref, wb_ref)):
        for n in range(2):
            out = times_dagger(link, [v_ref[2 * k + n] for k in range(6)])
            for k in range(6):
                w_ref[(2 * k + n) * ROWS : (2 * k + n + 1) * ROWS, :] = out[k]


def inner_body(v_ref, g_ref, acc_ref):
    link_y, link_z = plane_link(g_ref, 1), plane_link(g_ref, 2)

    def one(n, carry):
        field = [v_ref[2 * k + n] for k in range(6)]
        total = times(link_y, [y_next(x) for x in field])
        for part in (
            [y_prev(x) for x in times_dagger(link_y, field)],
            times(link_z, [z_next(x) for x in field]),
            [z_prev(x) for x in times_dagger(link_z, field)],
        ):
            total = [a + b for a, b in zip(total, part)]
        for k in range(6):
            acc_ref[2 * k + n] = total[k]
        return carry

    lax.fori_loop(0, 2, one, 0)


def summed(n, acc_ref, ahead_ref, behind_ref, link):
    hop = times(link, [ahead_ref[2 * k + n] for k in range(6)])
    return [
        acc_ref[2 * k + n] + hop[k] + behind_ref[pl.ds((2 * k + n) * ROWS, ROWS), :]
        for k in range(6)
    ]


def first_body(links_too, acc_ref, ahead_ref, behind_ref, g_ref, first_ref, w_ref):
    link = plane_link(g_ref, 0)

    def one(n, carry):
        first = [x / -6.0 for x in summed(n, acc_ref, ahead_ref, behind_ref, link)]
        out = times_dagger(link, first)
        for k in range(6):
            first_ref[2 * k + n] = first[k]
            w_ref[pl.ds((2 * k + n) * ROWS, ROWS), :] = out[k]
        return carry

    lax.fori_loop(0, 2, one, 0)
    if links_too:
        block = lax.axis_index("vec") // 2
        for n in range(18):
            at = 12 * ROWS + 2 * n
            w_ref[at : at + 2, :] = g_ref[n, pl.ds(2 * block, 2), :]
        w_ref[12 * ROWS + 36 :, :] = jnp.zeros((4, LANES), F32)


def filter_half(half, acc_ref, ahead_ref, behind_ref, v_ref, link, f_ref, half_ref):
    def one(n, carry):
        total = summed(n, acc_ref, ahead_ref, behind_ref, link)
        for k in range(6):
            f = total[k] / -3.0 - v_ref[2 * k + n]
            at = pl.ds((4 * k + 2 * half + n) * ROWS, ROWS)
            f_ref[at, :] = f
            if half_ref is not None:
                half_ref[at, :] = pltpu.roll(f, NZ, 1)
        return carry

    lax.fori_loop(0, 2, one, 0)


def second_body(
    edges, acca, aheada, behinda, va, accb, aheadb, behindb, vb, g_ref, out_ref, f_ref, half_ref
):
    link = plane_link(g_ref, 0)
    rolled = half_ref if edges else None
    filter_half(0, acca, aheada, behinda, va, link, f_ref, rolled)
    filter_half(1, accb, aheadb, behindb, vb, link, f_ref, rolled)
    low = lane_of((24, LANES)) < NZ
    for block in range(16):
        for q in range(2):
            out_ref[block, 24 * q : 24 * q + 24, :] = f_ref[pl.ds(2 * block + q, 24, ROWS), :]
        if not edges:
            continue
        under = half_ref[pl.ds((2 * block - 1) % ROWS, 24, ROWS), :]
        over = half_ref[pl.ds((2 * block + 2) % ROWS, 24, ROWS), :]
        out_ref[block, 48:72, :] = jnp.where(low, under, over)


def table_body(slabs, sc, mom, g_ref, behind_ref, m_ref, case_ref):
    first, second = lax.rem(sc[0], 3), lax.rem(sc[1], 3)
    along_x = (first == 0) | (second == 0)
    along_y = (first == 1) | (second == 1)
    case_ref[0] = along_x.astype(jnp.int32) + 2 * along_y.astype(jnp.int32)
    here = 4 * (lax.axis_index("vec") // 2)
    lane = lane_of((1, LANES))
    for op in range(NMOM):
        part_x = ((mom[op, 0] * lax.axis_index("space")) & (slabs - 1)).astype(F32) / slabs
        part_z = ((mom[op, 2] * (lane & (NZ - 1))) & (NZ - 1)).astype(F32) / NZ
        for q in range(2):
            row = here + 2 * q + lane // NZ
            part_y = ((mom[op, 1] * row) & (NY - 1)).astype(F32) / NY
            angle = (part_x + part_y + part_z) * (2.0 * math.pi)
            at = PHASES + 4 * op + q
            m_ref[at : at + 1, :] = jnp.cos(angle)
            m_ref[at + 2 : at + 3, :] = jnp.sin(angle)
    block = lax.axis_index("vec") // 2
    low = lane_of((1, LANES)) < NZ
    for op in range(NDISP):
        hop = lax.rem(sc[op] + 3, 6)
        direction = lax.rem(hop, 3)

        def put(reim, row, col, q, value):
            m_ref[pl.ds(((op * 18 + reim * 9 + row * 3 + col) * 2) + q, 1), :] = value

        @pl.when(hop < 3)
        def _():
            for n in range(18):
                for q in range(2):
                    m_ref[pl.ds((op * 18 + n) * 2 + q, 1), :] = g_ref[
                        direction * 18 + n, pl.ds(2 * block + q, 1), :
                    ]

        def dagger(rows_of):
            for reim in range(2):
                for row in range(3):
                    for col in range(3):
                        n = reim * 9 + col * 3 + row
                        for q in range(2):
                            value = rows_of(n, q)
                            put(reim, row, col, q, -value if reim else value)

        @pl.when(hop == 3)
        def _():
            dagger(lambda n, q: behind_ref[12 * ROWS + 2 * n + q : 12 * ROWS + 2 * n + q + 1, :])

        @pl.when(hop == 4)
        def _():
            def rows_of(n, q):
                under = g_ref[18 + n, pl.ds(lax.rem(2 * block + q + ROWS - 1, ROWS), 1), :]
                here = g_ref[18 + n, pl.ds(2 * block + q, 1), :]
                return pltpu.roll(jnp.where(low, here, under), NZ, 1)

            dagger(rows_of)

        @pl.when(hop == 5)
        def _():
            dagger(lambda n, q: z_prev(g_ref[36 + n, pl.ds(2 * block + q, 1), :]))


def rows_of_block(ref, tile, odd):
    both = ref[:, 8 * tile : 8 * tile + 8, :].reshape(8, 2, 8, LANES)
    left, right = both[:, 0], both[:, 1]
    low = lax.broadcasted_iota(jnp.int32, left.shape, 1) < 4
    if odd:
        mixed = jnp.where(low, pltpu.roll(left, 4, 1), right)
    else:
        mixed = jnp.where(low, left, pltpu.roll(right, 4, 1))
    return mixed.reshape(64, LANES)


def split(x):
    high = x.astype(jnp.bfloat16)
    return high, (x - high.astype(F32)).astype(jnp.bfloat16)


def gram_body(
    scale, along_x, along_y, sc, own_ref, other_ref, ahead_ref, behind_ref, m_ref,
    out_ref,
    f_ref, n_ref, lhs_hi, lhs_lo, rhs_hi, rhs_lo,
):
    core = lax.rem(lax.axis_index("vec"), 2)

    def column(k, q):
        return slice((2 * k + q) * LANES, (2 * k + q + 1) * LANES)

    def put_lhs(op, k, q, value):
        high, rest = split(value)
        lhs_hi[64 * op : 64 * op + 64, column(k, q)] = high
        lhs_lo[64 * op : 64 * op + 64, column(k, q)] = rest

    for q in range(2):
        for pair in range(3):
            tile = 3 * q + pair
            own = own_ref[:, 8 * tile : 8 * tile + 8, :]
            other = other_ref[:, 8 * tile : 8 * tile + 8, :]
            zero = jnp.where(core == 0, own, other)
            one = jnp.where(core == 0, other, own)
            low = lax.broadcasted_iota(jnp.int32, own.shape, 1) < 4
            even = jnp.where(low, zero, pltpu.roll(one, 4, 1)).reshape(128, LANES)
            odd = jnp.where(low, pltpu.roll(zero, 4, 1), one).reshape(128, LANES)
            for k, value in ((2 * pair, even), (2 * pair + 1, odd)):
                high, rest = split(value)
                for part, ref in ((high, rhs_hi), (rest, rhs_lo)):
                    ref[0:128, column(k, q)] = part
                    if k < 3:
                        ref[128:256, column(k + 3, q)] = -part
                    else:
                        ref[128:256, column(k - 3, q)] = part
            for odd_one in (0, 1):
                f_ref[2 * pair + odd_one, q] = rows_of_block(own_ref, tile, odd_one)
    for q in range(2):
        for op in range(NMOM):
            at = PHASES + 4 * op + q
            cosine, sine = m_ref[at : at + 1, :], m_ref[at + 2 : at + 3, :]
            for c in range(3):
                re, im = f_ref[c, q], f_ref[3 + c, q]
                put_lhs(op, c, q, cosine * re + sine * im)
                put_lhs(op, 3 + c, q, cosine * im - sine * re)
    low = lane_of((64, LANES)) < NZ
    for op in range(NDISP):
        hop = lax.rem(sc[op] + 3, 6)

        for which, ref in ((0, ahead_ref), (3, behind_ref)) if along_x else ():

            @pl.when(hop == which)
            def _():
                for k in range(6):
                    for q in range(2):
                        n_ref[k, q] = rows_of_block(ref, 3 * q + k // 2, k % 2)

        def y_ahead():
            for k in range(6):
                edge = rows_of_block(own_ref, 6 + k // 2, k % 2)
                here, over = pltpu.roll(f_ref[k, 0], NZ, 1), pltpu.roll(f_ref[k, 1], NZ, 1)
                n_ref[k, 0] = jnp.where(low, here, over)
                n_ref[k, 1] = jnp.where(low, over, edge)

        def y_behind():
            for k in range(6):
                edge = rows_of_block(own_ref, 6 + k // 2, k % 2)
                here, over = pltpu.roll(f_ref[k, 0], NZ, 1), pltpu.roll(f_ref[k, 1], NZ, 1)
                n_ref[k, 0] = jnp.where(low, edge, here)
                n_ref[k, 1] = jnp.where(low, here, over)

        if along_y:
            pl.when(hop == 1)(y_ahead)
            pl.when(hop == 4)(y_behind)

        @pl.when(hop == 2)
        def _():
            for k in range(6):
                for q in range(2):
                    n_ref[k, q] = z_next(f_ref[k, q])

        @pl.when(hop == 5)
        def _():
            for k in range(6):
                for q in range(2):
                    n_ref[k, q] = z_prev(f_ref[k, q])

        for q in range(2):

            def link(reim, row, col):
                at = (op * 18 + reim * 9 + row * 3 + col) * 2 + q
                return m_ref[at : at + 1, :]

            moved = times(link, [n_ref[k, q] for k in range(6)])
            for k in range(6):
                put_lhs(NMOM + op, k, q, moved[k])

    def dot(a, b):
        return lax.dot_general(
            a[...], b[...], (((1,), (1,)), ((), ())), preferred_element_type=F32
        )

    sums = dot(lhs_hi, rhs_hi) + (dot(lhs_hi, rhs_lo) + dot(lhs_lo, rhs_hi))
    tiles = [
        sums[64 * op : 64 * op + 64, 128 * reim : 128 * reim + 128] * scale
        for reim in range(2)
        for op in range(4)
    ]
    group = lane_of((64, LANES)) // 16
    for bit in (4, 2, 1):
        clear = lax.rem(group // bit, 2) == 0
        for i in range(8):
            if i & bit == 0:
                a, b = tiles[i], tiles[i + bit]
                tiles[i] = jnp.where(clear, a, pltpu.roll(b, 16 * bit, 1))
                tiles[i + bit] = jnp.where(clear, pltpu.roll(a, LANES - 16 * bit, 1), b)
    for slab in range(8):
        out_ref[slab] = tiles[slab]


def finish_body(part_ref, out_ref):
    parts = [part_ref[8 * i : 8 * i + 8, :] for i in range(64)]
    while len(parts) > 1:
        parts = [a + b for a, b in zip(parts[::2], parts[1::2])]
    total = parts[0] + pltpu.roll(parts[0], 4, 0)
    for t in range(8):
        moved = total if t == 0 else pltpu.roll(total, LANES - 16 * t, 1)
        out_ref[t] = moved[:4, :16]


def local(slabs, vecs, vectors, gauge_links, momenta, displacements):
    field_bytes = 24 * ROWS * LANES * 4
    field = vectors.reshape(24, ROWS, LANES)
    gauge = gauge_links.reshape(54, ROWS, LANES)
    up = [(i, (i + 1) % slabs) for i in range(slabs)]
    down = [(i, (i - 1) % slabs) for i in range(slabs)]
    partner = [(i, i ^ 1) for i in range(vecs)]
    cores = [[2 * i + c for i in range(vecs // 2)] for c in range(2)]
    alike = [[2 * i + c for i in range(slabs * vecs // 2)] for c in range(2)]

    half = struct(12, ROWS, LANES)
    rows = struct(12 * ROWS, LANES)
    va, vb, wa, wb = call(
        start_body,
        [half, half, rows, rows],
        "hh",
        scratch=[VMEM((18, ROWS, LANES), F32), pltpu.SemaphoreType.DMA((18,))],
        flops=3 << 20,
        nbytes=3 * field_bytes,
    )(field, gauge)
    inner = call(inner_body, half, "vv", flops=6 << 20, nbytes=3 * field_bytes)

    def step(links_too, *operands):
        w = struct(12 * ROWS + 40, LANES) if links_too else rows
        body = functools.partial(first_body, links_too)
        return call(body, [half, w], "vvvx", flops=3 << 20, nbytes=3 * field_bytes)(*operands)

    def exchange(v, w):
        return lax.ppermute(v, "space", down), lax.ppermute(w, "space", up)

    aheada, behinda = exchange(va, wa)
    aheadb, behindb = exchange(vb, wb)
    firsta, wa = step(True, inner(va, gauge), aheada, behinda, gauge)
    ahead2a, behind2a = exchange(firsta, wa)
    firstb, wb = step(False, inner(vb, gauge), aheadb, behindb, gauge)
    ahead2b, behind2b = exchange(firstb, wb)
    acca, accb = inner(firsta, gauge), inner(firstb, gauge)
    table, case = call(
        functools.partial(table_body, slabs),
        [struct(PHASES + 4 * NMOM, LANES), jax.ShapeDtypeStruct((1,), jnp.int32)],
        "ssvv",
        flops=1 << 20,
        nbytes=4 * field_bytes,
    )(displacements, momenta, gauge, behind2a)
    acca, accb, table, case = lax.optimization_barrier((acca, accb, table, case))
    scale = 1.0 / math.sqrt(3 * slabs * NY * NZ)

    def elementals(along_x, along_y, fields, gauge, table):
        cut = call(
            functools.partial(second_body, along_y),
            struct(16, 72 if along_y else 48, LANES),
            "vvvvvvvvx",
            scratch=[VMEM((24 * ROWS, LANES), F32)] * 2,
            flops=6 << 20,
            nbytes=7 * field_bytes,
        )(*fields, gauge)
        own = lax.all_to_all(cut, "vec", 0, 0, axis_index_groups=cores)
        bulk = own[:, :48]
        ahead3 = behind3 = bulk
        if along_x:
            ahead3 = lax.ppermute(bulk, "space", down)
            behind3 = lax.ppermute(bulk, "space", up)
        other = lax.ppermute(bulk, "vec", partner)
        sums = call(
            functools.partial(gram_body, scale, along_x, along_y),
            struct(slabs, 64, LANES),
            "svvvvv",
            scratch=[VMEM((6, 2, 64, LANES), F32)] * 2
            + [VMEM((256, 12 * LANES), jnp.bfloat16)] * 4,
            room=16,
            flops=600 << 20,
            nbytes=6 * field_bytes,
        )(displacements, own, other, ahead3, behind3, table)
        sums = sums.reshape(slabs * vecs // 2, 4, LANES)
        parts = lax.all_to_all(sums, ("space", "vec"), 0, 0, axis_index_groups=alike)
        return call(finish_body, struct(8, 4, 16), "v")(parts.reshape(512, LANES))

    out = lax.switch(
        case[0],
        [
            functools.partial(elementals, bool(i & 1), bool(i & 2))
            for i in range(4)
        ],
        (acca, ahead2a, behind2a, va, accb, ahead2b, behind2b, vb),
        gauge,
        table,
    )
    return out.reshape(2, 4, 4, 16)


def solution(mesh):
    placed = (
        P(None, None, "vec", "space", None),
        P(None, None, None, None, "space", None),
        P(),
        P(),
    )
    body = functools.partial(local, mesh.shape["space"], mesh.shape["vec"])
    return jax.shard_map(
        body, mesh=mesh, in_specs=placed, out_specs=P(None, None, "vec", "space"), check_vma=False
    )
```

```python
import functools
import math

import jax
import jax.numpy as jnp
from jax import lax
from jax.experimental import pallas as pl
from jax.experimental.pallas import tpu as pltpu
from jax.sharding import PartitionSpec as P

NY = 64
NZ = 64
NMOM = 2
NDISP = 2
ROWS = 32
LANES = 128
CASES = ((False, 0), (True, 0), (False, 1), (True, 1), (False, 2))
PHASES = 36 * NDISP
VMEM = pltpu.VMEM
F32 = jnp.float32


LINKS = pl.BlockSpec((18, ROWS, LANES), lambda i: (0, 0, 0))


SMEM_BLOCK = pl.BlockSpec(memory_space=pltpu.SMEM)


def call(body, out_shape, ins, scratch=(), flops=0, nbytes=0, room=8192):
    kinds = {
        "s": SMEM_BLOCK,
        "x": LINKS,
        "v": pl.BlockSpec(memory_space=VMEM),
        "h": pl.BlockSpec(memory_space=pl.ANY),
    }
    specs = [kinds[letter] for letter in ins]
    many = isinstance(out_shape, (list, tuple))
    return pl.pallas_call(
        body,
        out_shape=out_shape,
        grid=(1,) if "x" in ins else (),
        in_specs=specs,
        out_specs=[
            pl.BlockSpec(memory_space=VMEM) if each.dtype != jnp.int32 else SMEM_BLOCK
            for each in out_shape
        ]
        if many
        else pl.BlockSpec(memory_space=VMEM),
        scratch_shapes=list(scratch),
        cost_estimate=pl.CostEstimate(flops=flops, bytes_accessed=nbytes, transcendentals=0),
        compiler_params=pltpu.CompilerParams(vmem_limit_bytes=room << 10),
    )


def struct(*shape):
    return jax.ShapeDtypeStruct(shape, F32)


def times(link, field):
    out = []
    for i in range(3):
        re = im = None
        for j in range(3):
            a, b = link(0, i, j), link(1, i, j)
            x, y = field[j], field[3 + j]
            re_j, im_j = a * x - b * y, a * y + b * x
            re = re_j if re is None else re + re_j
            im = im_j if im is None else im + im_j
        out.append((re, im))
    return [o[0] for o in out] + [o[1] for o in out]


def times_dagger(link, field):
    out = []
    for i in range(3):
        re = im = None
        for j in range(3):
            a, b = link(0, j, i), link(1, j, i)
            x, y = field[j], field[3 + j]
            re_j, im_j = a * x + b * y, a * y - b * x
            re = re_j if re is None else re + re_j
            im = im_j if im is None else im + im_j
        out.append((re, im))
    return [o[0] for o in out] + [o[1] for o in out]


def lane_of(shape):
    return lax.broadcasted_iota(jnp.int32, shape, len(shape) - 1)


def z_next(x):
    axis = x.ndim - 1
    end = lane_of(x.shape) % NZ == NZ - 1
    return jnp.where(end, pltpu.roll(x, NZ - 1, axis), pltpu.roll(x, LANES - 1, axis))


def z_prev(x):
    axis = x.ndim - 1
    start = lane_of(x.shape) % NZ == 0
    return jnp.where(start, pltpu.roll(x, LANES - NZ + 1, axis), pltpu.roll(x, 1, axis))


def y_next(x):
    half = pltpu.roll(x, NZ, 1)
    return jnp.where(lane_of(x.shape) < NZ, half, pltpu.roll(half, ROWS - 1, 0))


def y_prev(x):
    half = pltpu.roll(x, NZ, 1)
    return jnp.where(lane_of(x.shape) < NZ, pltpu.roll(half, 1, 0), half)


def plane_link(g_ref, direction):
    return lambda reim, row, col: g_ref[direction * 18 + reim * 9 + row * 3 + col]


def start_body(v_hbm, g_hbm, va_ref, vb_ref, wa_ref, wb_ref, g_ref, sems):
    copies = []
    for i in range(6):
        for half, v_ref in enumerate((va_ref, vb_ref)):
            copies.append(
                pltpu.make_async_copy(
                    v_hbm.at[pl.ds(4 * i + 2 * half, 2)],
                    v_ref.at[pl.ds(2 * i, 2)],
                    sems.at[2 * i + half],
                )
            )
        copies.append(
            pltpu.make_async_copy(
                g_hbm.at[pl.ds(3 * i, 3)], g_ref.at[pl.ds(3 * i, 3)], sems.at[12 + i]
            )
        )
    for copy in copies:
        copy.start()
    for copy in copies:
        copy.wait()
    link = plane_link(g_ref, 0)
    for v_ref, w_ref in ((va_ref, wa_ref), (vb_ref, wb_ref)):
        for n in range(2):
            out = times_dagger(link, [v_ref[2 * k + n] for k in range(6)])
            for k in range(6):
                w_ref[(2 * k + n) * ROWS : (2 * k + n + 1) * ROWS, :] = out[k]


def inner_body(v_ref, g_ref, acc_ref):
    link_y, link_z = plane_link(g_ref, 1), plane_link(g_ref, 2)

    def one(n, carry):
        field = [v_ref[2 * k + n] for k in range(6)]
        total = times(link_y, [y_next(x) for x in field])
        for part in (
            [y_prev(x) for x in times_dagger(link_y, field)],
            times(link_z, [z_next(x) for x in field]),
            [z_prev(x) for x in times_dagger(link_z, field)],
        ):
            total = [a + b for a, b in zip(total, part)]
        for k in range(6):
            acc_ref[2 * k + n] = total[k]
        return carry

    lax.fori_loop(0, 2, one, 0)


def summed(n, acc_ref, ahead_ref, behind_ref, link):
    hop = times(link, [ahead_ref[2 * k + n] for k in range(6)])
    return [
        acc_ref[2 * k + n] + hop[k] + behind_ref[pl.ds((2 * k + n) * ROWS, ROWS), :]
        for k in range(6)
    ]


def first_body(links_too, acc_ref, ahead_ref, behind_ref, g_ref, first_ref, w_ref):
    link = plane_link(g_ref, 0)

    def one(n, carry):
        first = [x / -6.0 for x in summed(n, acc_ref, ahead_ref, behind_ref, link)]
        out = times_dagger(link, first)
        for k in range(6):
            first_ref[2 * k + n] = first[k]
            w_ref[pl.ds((2 * k + n) * ROWS, ROWS), :] = out[k]
        return carry

    lax.fori_loop(0, 2, one, 0)
    if links_too:
        block = lax.axis_index("vec") // 2
        for n in range(18):
            at = 12 * ROWS + 2 * n
            w_ref[at : at + 2, :] = g_ref[n, pl.ds(2 * block, 2), :]
        w_ref[12 * ROWS + 36 :, :] = jnp.zeros((4, LANES), F32)


def filter_half(half, acc_ref, ahead_ref, behind_ref, v_ref, link, f_ref, half_ref):
    def one(n, carry):
        total = summed(n, acc_ref, ahead_ref, behind_ref, link)
        for k in range(6):
            f = total[k] / -3.0 - v_ref[2 * k + n]
            at = pl.ds((4 * k + 2 * half + n) * ROWS, ROWS)
            f_ref[at, :] = f
            if half_ref is not None:
                half_ref[at, :] = pltpu.roll(f, NZ, 1)
        return carry

    lax.fori_loop(0, 2, one, 0)


def row_hop(sc, op):
    return lax.rem(sc[op] + 3, 6)


def second_body(
    sides, sc, acca, aheada, behinda, va, accb, aheadb, behindb, vb, g_ref, out_ref, f_ref, half_ref
):
    link = plane_link(g_ref, 0)
    rolled = half_ref if sides else None
    filter_half(0, acca, aheada, behinda, va, link, f_ref, rolled)
    filter_half(1, accb, aheadb, behindb, vb, link, f_ref, rolled)

    def cut(block, edge):
        for q in range(2):
            out_ref[block, 24 * q : 24 * q + 24, :] = f_ref[pl.ds(2 * block + q, 24, ROWS), :]
        under, over = (2 * block - 1) % ROWS, (2 * block + 2) % ROWS
        if edge is None:
            return
        if edge == "two":
            low = lane_of((24, LANES)) < NZ
            both = half_ref[pl.ds(under, 24, ROWS), :], half_ref[pl.ds(over, 24, ROWS), :]
            out_ref[block, 48:72, :] = jnp.where(low, *both)
            return
        low = lane_of((12, LANES)) < NZ
        at, near, far = (over, f_ref, half_ref) if edge == "over" else (under, half_ref, f_ref)
        packed = near[pl.ds(at, 12, ROWS), :], far[pl.ds(at + 12 * ROWS, 12, ROWS), :]
        out_ref[block, 48:60, :] = jnp.where(low, *packed)
        out_ref[block, 60:64, :] = jnp.zeros((4, LANES), F32)

    def cut_all(edge):
        for block in range(16):
            cut(block, edge)

    if sides != 1:
        cut_all("two" if sides else None)
    else:
        over = (row_hop(sc, 0) == 1) | (row_hop(sc, 1) == 1)
        pl.when(over)(lambda: cut_all("over"))
        pl.when(jnp.logical_not(over))(lambda: cut_all("under"))


def table_body(slabs, sc, mom, g_ref, behind_ref, m_ref, case_ref):
    hops = row_hop(sc, 0), row_hop(sc, 1)
    down, over, up, under = (
        ((hops[0] == h) | (hops[1] == h)).astype(jnp.int32) for h in (0, 1, 3, 4)
    )
    case_ref[0] = jnp.where(over + under == 2, 4, (down | up) + 2 * (over | under))
    here = 4 * (lax.axis_index("vec") // 2)
    lane = lane_of((1, LANES))
    for op in range(NMOM):
        part_x = ((mom[op, 0] * lax.axis_index("space")) & (slabs - 1)).astype(F32) / slabs
        part_z = ((mom[op, 2] * (lane & (NZ - 1))) & (NZ - 1)).astype(F32) / NZ
        for q in range(2):
            row = here + 2 * q + lane // NZ
            part_y = ((mom[op, 1] * row) & (NY - 1)).astype(F32) / NY
            angle = (part_x + part_y + part_z) * (2.0 * math.pi)
            at = PHASES + 4 * op + q
            m_ref[at : at + 1, :] = jnp.cos(angle)
            m_ref[at + 2 : at + 3, :] = jnp.sin(angle)
    block = lax.axis_index("vec") // 2
    low = lane_of((1, LANES)) < NZ
    for op in range(NDISP):
        hop = row_hop(sc, op)
        direction = lax.rem(hop, 3)

        def put(reim, row, col, q, value):
            m_ref[pl.ds(((op * 18 + reim * 9 + row * 3 + col) * 2) + q, 1), :] = value

        @pl.when(hop < 3)
        def _():
            for n in range(18):
                for q in range(2):
                    m_ref[pl.ds((op * 18 + n) * 2 + q, 1), :] = g_ref[
                        direction * 18 + n, pl.ds(2 * block + q, 1), :
                    ]

        def dagger(rows_of):
            for reim in range(2):
                for row in range(3):
                    for col in range(3):
                        n = reim * 9 + col * 3 + row
                        for q in range(2):
                            value = rows_of(n, q)
                            put(reim, row, col, q, -value if reim else value)

        @pl.when(hop == 3)
        def _():
            dagger(lambda n, q: behind_ref[12 * ROWS + 2 * n + q : 12 * ROWS + 2 * n + q + 1, :])

        @pl.when(hop == 4)
        def _():
            def rows_of(n, q):
                under = g_ref[18 + n, pl.ds(lax.rem(2 * block + q + ROWS - 1, ROWS), 1), :]
                here = g_ref[18 + n, pl.ds(2 * block + q, 1), :]
                return pltpu.roll(jnp.where(low, here, under), NZ, 1)

            dagger(rows_of)

        @pl.when(hop == 5)
        def _():
            dagger(lambda n, q: z_prev(g_ref[36 + n, pl.ds(2 * block + q, 1), :]))


def rows_of_block(ref, tile, odd):
    both = ref[:, 8 * tile : 8 * tile + 8, :].reshape(8, 2, 8, LANES)
    left, right = both[:, 0], both[:, 1]
    low = lax.broadcasted_iota(jnp.int32, left.shape, 1) < 4
    if odd:
        mixed = jnp.where(low, pltpu.roll(left, 4, 1), right)
    else:
        mixed = jnp.where(low, left, pltpu.roll(right, 4, 1))
    return mixed.reshape(64, LANES)


def split(x):
    high = x.astype(jnp.bfloat16)
    return high, (x - high.astype(F32)).astype(jnp.bfloat16)


def gram_body(
    scale, along_x, sides, sc, own_ref, other_ref, ahead_ref, behind_ref, m_ref,
    out_ref, f_ref, n_ref, lhs, rhs,
):
    core = lax.rem(lax.axis_index("vec"), 2)

    def column(k, q):
        return slice((2 * k + q) * LANES, (2 * k + q + 1) * LANES)

    def put_lhs(op, k, q, value):
        high, rest = split(value)
        at = slice(64 * op, 64 * op + 64)
        lhs[0, at, column(k, q)] = high
        lhs[1, at, column(k, q)] = rest

    for q in range(2):
        for pair in range(3):
            tile = 3 * q + pair
            own = own_ref[:, 8 * tile : 8 * tile + 8, :]
            other = other_ref[:, 8 * tile : 8 * tile + 8, :]
            zero = jnp.where(core == 0, own, other)
            one = jnp.where(core == 0, other, own)
            low = lax.broadcasted_iota(jnp.int32, own.shape, 1) < 4
            even = jnp.where(low, zero, pltpu.roll(one, 4, 1)).reshape(128, LANES)
            odd = jnp.where(low, pltpu.roll(zero, 4, 1), one).reshape(128, LANES)
            for k, value in ((2 * pair, even), (2 * pair + 1, odd)):
                high, rest = split(value)
                for which, part in ((0, high), (1, rest)):
                    rhs[which, 0:128, column(k, q)] = part
                    if k < 3:
                        rhs[which, 128:256, column(k + 3, q)] = -part
                    else:
                        rhs[which, 128:256, column(k - 3, q)] = part
            for odd_one in (0, 1):
                f_ref[2 * pair + odd_one, q] = rows_of_block(own_ref, tile, odd_one)
    def phase(op, carry):
        for q in range(2):
            at = PHASES + 4 * op + q
            cosine, sine = m_ref[pl.ds(at, 1), :], m_ref[pl.ds(at + 2, 1), :]
            for c in range(3):
                re, im = f_ref[c, q], f_ref[3 + c, q]
                put_lhs(op, c, q, cosine * re + sine * im)
                put_lhs(op, 3 + c, q, cosine * im - sine * re)
        return carry

    for op in range(NMOM):
        phase(op, 0)
    low = lane_of((64, LANES)) < NZ
    def displace(op, carry):
        hop = row_hop(sc, op)

        for which, ref in ((0, ahead_ref), (3, behind_ref)) if along_x else ():

            @pl.when(hop == which)
            def _():
                for k in range(6):
                    for q in range(2):
                        n_ref[k, q] = rows_of_block(ref, 3 * q + k // 2, k % 2)

        def edge(k, hop):
            if sides == 2:
                return rows_of_block(own_ref, 6 + k // 2, k % 2)
            packed = rows_of_block(own_ref, 6 + (k % 3) // 2, (k % 3) % 2)
            return packed if (k < 3) == (hop == 4) else pltpu.roll(packed, NZ, 1)

        for which in (1, 4) if sides else ():

            @pl.when(hop == which)
            def _():
                for k in range(6):
                    here, over = pltpu.roll(f_ref[k, 0], NZ, 1), pltpu.roll(f_ref[k, 1], NZ, 1)
                    if which == 1:
                        n_ref[k, 0] = jnp.where(low, here, over)
                        n_ref[k, 1] = jnp.where(low, over, edge(k, which))
                    else:
                        n_ref[k, 0] = jnp.where(low, edge(k, which), here)
                        n_ref[k, 1] = jnp.where(low, here, over)

        @pl.when(hop == 2)
        def _():
            for k in range(6):
                for q in range(2):
                    n_ref[k, q] = z_next(f_ref[k, q])

        @pl.when(hop == 5)
        def _():
            for k in range(6):
                for q in range(2):
                    n_ref[k, q] = z_prev(f_ref[k, q])

        for q in range(2):

            def link(reim, row, col):
                at = (op * 18 + reim * 9 + row * 3 + col) * 2 + q
                return m_ref[pl.ds(at, 1), :]

            moved = times(link, [n_ref[k, q] for k in range(6)])
            for k in range(6):
                put_lhs(NMOM + op, k, q, moved[k])
        return carry

    for op in range(NDISP):
        displace(op, 0)
    def dot(i, j):
        return lax.dot_general(
            lhs[i], rhs[j], (((1,), (1,)), ((), ())), preferred_element_type=F32
        )

    sums = dot(0, 0) + (dot(0, 1) + dot(1, 0))
    tiles = [
        sums[64 * op : 64 * op + 64, 128 * reim : 128 * reim + 128] * scale
        for reim in range(2)
        for op in range(4)
    ]
    group = lane_of((64, LANES)) // 16
    for bit in (4, 2, 1):
        clear = lax.rem(group // bit, 2) == 0
        for i in range(8):
            if i & bit == 0:
                a, b = tiles[i], tiles[i + bit]
                tiles[i] = jnp.where(clear, a, pltpu.roll(b, 16 * bit, 1))
                tiles[i + bit] = jnp.where(clear, pltpu.roll(a, LANES - 16 * bit, 1), b)
    for slab in range(8):
        out_ref[slab] = tiles[slab]


def finish_body(part_ref, out_ref):
    parts = [part_ref[8 * i : 8 * i + 8, :] for i in range(64)]
    while len(parts) > 1:
        parts = [a + b for a, b in zip(parts[::2], parts[1::2])]
    total = parts[0] + pltpu.roll(parts[0], 4, 0)
    for t in range(8):
        moved = total if t == 0 else pltpu.roll(total, LANES - 16 * t, 1)
        out_ref[t] = moved[:4, :16]


def local(slabs, vecs, vectors, gauge_links, momenta, displacements):
    field_bytes = 24 * ROWS * LANES * 4
    field = vectors.reshape(24, ROWS, LANES)
    gauge = gauge_links.reshape(54, ROWS, LANES)
    up = [(i, (i + 1) % slabs) for i in range(slabs)]
    down = [(i, (i - 1) % slabs) for i in range(slabs)]
    partner = [(i, i ^ 1) for i in range(vecs)]
    cores = [[2 * i + c for i in range(vecs // 2)] for c in range(2)]
    alike = [[2 * i + c for i in range(slabs * vecs // 2)] for c in range(2)]

    half = struct(12, ROWS, LANES)
    rows = struct(12 * ROWS, LANES)
    va, vb, wa, wb = call(
        start_body,
        [half, half, rows, rows],
        "hh",
        scratch=[VMEM((18, ROWS, LANES), F32), pltpu.SemaphoreType.DMA((18,))],
        flops=3 << 20,
        nbytes=3 * field_bytes,
        room=63400,
    )(field, gauge)
    inner = call(inner_body, half, "vv", flops=6 << 20, nbytes=3 * field_bytes)

    def step(links_too, *operands):
        w = struct(12 * ROWS + 40, LANES) if links_too else rows
        body = functools.partial(first_body, links_too)
        return call(body, [half, w], "vvvx", flops=3 << 20, nbytes=3 * field_bytes)(*operands)

    def exchange(v, w):
        return lax.ppermute(v, "space", down), lax.ppermute(w, "space", up)

    aheada, behinda = exchange(va, wa)
    aheadb, behindb = exchange(vb, wb)
    firsta, wa = step(True, inner(va, gauge), aheada, behinda, gauge)
    ahead2a, behind2a = exchange(firsta, wa)
    firstb, wb = step(False, inner(vb, gauge), aheadb, behindb, gauge)
    ahead2b, behind2b = exchange(firstb, wb)
    acca, accb = inner(firsta, gauge), inner(firstb, gauge)
    table, case = call(
        functools.partial(table_body, slabs),
        [struct(PHASES + 4 * NMOM, LANES), jax.ShapeDtypeStruct((1,), jnp.int32)],
        "ssvv",
        flops=1 << 20,
        nbytes=4 * field_bytes,
    )(displacements, momenta, gauge, behind2a)
    acca, accb, table, case = lax.optimization_barrier((acca, accb, table, case))
    scale = 1.0 / math.sqrt(3 * slabs * NY * NZ)

    def partial_sums(along_x, sides, fields, gauge, table):
        cut = call(
            functools.partial(second_body, sides),
            struct(16, (48, 64, 72)[sides], LANES),
            "svvvvvvvvx",
            scratch=[VMEM((24 * ROWS, LANES), F32)] * 2,
            flops=6 << 20,
            nbytes=7 * field_bytes,
        )(displacements, *fields, gauge)
        own = lax.all_to_all(cut, "vec", 0, 0, axis_index_groups=cores)
        bulk = own[:, :48]
        ahead = lax.ppermute(bulk, "space", down) if along_x else bulk
        behind = lax.ppermute(bulk, "space", up) if along_x else bulk
        other = lax.ppermute(bulk, "vec", partner)
        return call(
            functools.partial(gram_body, scale, along_x, sides),
            struct(slabs, 64, LANES),
            "svvvvv",
            scratch=[VMEM((6, 2, 64, LANES), F32)] * 2
            + [VMEM((2, 256, 12 * LANES), jnp.bfloat16)] * 2,
            room=16384,
            flops=600 << 20,
            nbytes=6 * field_bytes,
        )(displacements, own, other, ahead, behind, table)

    sums = lax.switch(
        case[0],
        [functools.partial(partial_sums, *case_of) for case_of in CASES],
        (acca, ahead2a, behind2a, va, accb, ahead2b, behind2b, vb),
        gauge,
        table,
    )
    sums = sums.reshape(slabs * vecs // 2, 4, LANES)
    parts = lax.all_to_all(sums, ("space", "vec"), 0, 0, axis_index_groups=alike)
    out = call(finish_body, struct(8, 4, 16), "v")(parts.reshape(512, LANES))
    return out.reshape(2, 4, 4, 16)


def solution(mesh):
    placed = (
        P(None, None, "vec", "space", None),
        P(None, None, None, None, "space", None),
        P(),
        P(),
    )
    body = functools.partial(local, mesh.shape["space"], mesh.shape["vec"])
    return jax.shard_map(
        body, mesh=mesh, in_specs=placed, out_specs=P(None, None, "vec", "space"), check_vma=False
    )
```

```python
import functools
import math

import jax
import jax.numpy as jnp
from jax import lax
from jax.experimental import pallas as pl
from jax.experimental.pallas import tpu as pltpu
from jax.sharding import PartitionSpec as P

NY = 64
NZ = 64
NMOM = 2
NDISP = 2
ROWS = 32
LANES = 128
CASES = ((False, 0), (True, 0), (False, 1), (True, 1), (False, 2))
PHASES = 36 * NDISP
HOPS = PHASES + 4 * NMOM
VMEM = pltpu.VMEM
F32 = jnp.float32


LINKS = pl.BlockSpec((18, ROWS, LANES), lambda i: (0, 0, 0))


SMEM_BLOCK = pl.BlockSpec(memory_space=pltpu.SMEM)


def call(body, out_shape, ins, scratch=(), flops=0, nbytes=0, room=8192):
    kinds = {
        "s": SMEM_BLOCK,
        "x": LINKS,
        "v": pl.BlockSpec(memory_space=VMEM),
        "h": pl.BlockSpec(memory_space=pl.ANY),
    }
    specs = [kinds[letter] for letter in ins]
    many = isinstance(out_shape, (list, tuple))
    return pl.pallas_call(
        body,
        out_shape=out_shape,
        grid=(1,) if "x" in ins else (),
        in_specs=specs,
        out_specs=[
            pl.BlockSpec(memory_space=VMEM) if each.dtype != jnp.int32 else SMEM_BLOCK
            for each in out_shape
        ]
        if many
        else pl.BlockSpec(memory_space=VMEM),
        scratch_shapes=list(scratch),
        cost_estimate=pl.CostEstimate(flops=flops, bytes_accessed=nbytes, transcendentals=0),
        compiler_params=pltpu.CompilerParams(vmem_limit_bytes=room << 10),
    )


def struct(*shape):
    return jax.ShapeDtypeStruct(shape, F32)


def times(link, field):
    out = []
    for i in range(3):
        re = im = None
        for j in range(3):
            a, b = link(0, i, j), link(1, i, j)
            x, y = field[j], field[3 + j]
            re_j, im_j = a * x - b * y, a * y + b * x
            re = re_j if re is None else re + re_j
            im = im_j if im is None else im + im_j
        out.append((re, im))
    return [o[0] for o in out] + [o[1] for o in out]


def times_dagger(link, field):
    out = []
    for i in range(3):
        re = im = None
        for j in range(3):
            a, b = link(0, j, i), link(1, j, i)
            x, y = field[j], field[3 + j]
            re_j, im_j = a * x + b * y, a * y - b * x
            re = re_j if re is None else re + re_j
            im = im_j if im is None else im + im_j
        out.append((re, im))
    return [o[0] for o in out] + [o[1] for o in out]


def lane_of(shape):
    return lax.broadcasted_iota(jnp.int32, shape, len(shape) - 1)


def z_next(x):
    axis = x.ndim - 1
    end = lane_of(x.shape) % NZ == NZ - 1
    return jnp.where(end, pltpu.roll(x, NZ - 1, axis), pltpu.roll(x, LANES - 1, axis))


def z_prev(x):
    axis = x.ndim - 1
    start = lane_of(x.shape) % NZ == 0
    return jnp.where(start, pltpu.roll(x, LANES - NZ + 1, axis), pltpu.roll(x, 1, axis))


def y_next(x):
    half = pltpu.roll(x, NZ, 1)
    return jnp.where(lane_of(x.shape) < NZ, half, pltpu.roll(half, ROWS - 1, 0))


def y_prev(x):
    half = pltpu.roll(x, NZ, 1)
    return jnp.where(lane_of(x.shape) < NZ, pltpu.roll(half, 1, 0), half)


def plane_link(g_ref, direction):
    return lambda reim, row, col: g_ref[direction * 18 + reim * 9 + row * 3 + col]


def start_body(v_hbm, g_hbm, va_ref, vb_ref, wa_ref, wb_ref, g_ref, sems):
    copies = []
    for i in range(6):
        for half, v_ref in enumerate((va_ref, vb_ref)):
            copies.append(
                pltpu.make_async_copy(
                    v_hbm.at[pl.ds(4 * i + 2 * half, 2)],
                    v_ref.at[pl.ds(2 * i, 2)],
                    sems.at[2 * i + half],
                )
            )
        copies.append(
            pltpu.make_async_copy(
                g_hbm.at[pl.ds(3 * i, 3)], g_ref.at[pl.ds(3 * i, 3)], sems.at[12 + i]
            )
        )
    for copy in copies:
        copy.start()
    for copy in copies:
        copy.wait()
    link = plane_link(g_ref, 0)
    for v_ref, w_ref in ((va_ref, wa_ref), (vb_ref, wb_ref)):
        for n in range(2):
            out = times_dagger(link, [v_ref[2 * k + n] for k in range(6)])
            for k in range(6):
                w_ref[(2 * k + n) * ROWS : (2 * k + n + 1) * ROWS, :] = out[k]


def inner_body(v_ref, g_ref, acc_ref):
    link_y, link_z = plane_link(g_ref, 1), plane_link(g_ref, 2)

    def one(n, carry):
        field = [v_ref[2 * k + n] for k in range(6)]
        total = times(link_y, [y_next(x) for x in field])
        for part in (
            [y_prev(x) for x in times_dagger(link_y, field)],
            times(link_z, [z_next(x) for x in field]),
            [z_prev(x) for x in times_dagger(link_z, field)],
        ):
            total = [a + b for a, b in zip(total, part)]
        for k in range(6):
            acc_ref[2 * k + n] = total[k]
        return carry

    lax.fori_loop(0, 2, one, 0)


def summed(n, acc_ref, ahead_ref, behind_ref, link):
    hop = times(link, [ahead_ref[2 * k + n] for k in range(6)])
    return [
        acc_ref[2 * k + n] + hop[k] + behind_ref[pl.ds((2 * k + n) * ROWS, ROWS), :]
        for k in range(6)
    ]


def first_body(links_too, acc_ref, ahead_ref, behind_ref, g_ref, first_ref, w_ref):
    link = plane_link(g_ref, 0)

    def one(n, carry):
        first = [x / -6.0 for x in summed(n, acc_ref, ahead_ref, behind_ref, link)]
        out = times_dagger(link, first)
        for k in range(6):
            first_ref[2 * k + n] = first[k]
            w_ref[pl.ds((2 * k + n) * ROWS, ROWS), :] = out[k]
        return carry

    lax.fori_loop(0, 2, one, 0)
    if links_too:
        block = lax.axis_index("vec") // 2
        for n in range(18):
            at = 12 * ROWS + 2 * n
            w_ref[at : at + 2, :] = g_ref[n, pl.ds(2 * block, 2), :]
        w_ref[12 * ROWS + 36 :, :] = jnp.zeros((4, LANES), F32)


def filter_half(half, acc_ref, ahead_ref, behind_ref, v_ref, link, f_ref, half_ref):
    def one(n, carry):
        total = summed(n, acc_ref, ahead_ref, behind_ref, link)
        for k in range(6):
            f = total[k] / -3.0 - v_ref[2 * k + n]
            at = pl.ds((4 * k + 2 * half + n) * ROWS, ROWS)
            f_ref[at, :] = f
            if half_ref is not None:
                half_ref[at, :] = pltpu.roll(f, NZ, 1)
        return carry

    lax.fori_loop(0, 2, one, 0)


def row_hop(sc, op):
    return lax.rem(sc[op] + 3, 6)


def second_body(
    sides, m_ref, acca, aheada, behinda, va, accb, aheadb, behindb, vb, g_ref,
    out_ref, f_ref, half_ref,
):
    link = plane_link(g_ref, 0)
    rolled = half_ref if sides else None
    filter_half(0, acca, aheada, behinda, va, link, f_ref, rolled)
    filter_half(1, accb, aheadb, behindb, vb, link, f_ref, rolled)

    def cut(block, edge):
        for q in range(2):
            out_ref[block, 24 * q : 24 * q + 24, :] = f_ref[pl.ds(2 * block + q, 24, ROWS), :]
        under, over = (2 * block - 1) % ROWS, (2 * block + 2) % ROWS
        if edge is None:
            return
        if edge == "two":
            low = lane_of((24, LANES)) < NZ
            both = half_ref[pl.ds(under, 24, ROWS), :], half_ref[pl.ds(over, 24, ROWS), :]
            out_ref[block, 48:72, :] = jnp.where(low, *both)
            return
        low = lane_of((12, LANES)) < NZ

        def rows(ref, at):
            return ref[pl.ds(at, 12, ROWS), :]

        above = jnp.where(low, rows(f_ref, over), rows(half_ref, over + 12 * ROWS))
        below = jnp.where(low, rows(half_ref, under), rows(f_ref, under + 12 * ROWS))
        out_ref[block, 48:60, :] = jnp.where(m_ref[HOPS + 2 : HOPS + 3, :] > 0.5, above, below)
        out_ref[block, 60:64, :] = jnp.zeros((4, LANES), F32)

    for block in range(16):
        cut(block, (None, "one", "two")[sides])


def table_body(slabs, sc, mom, g_ref, behind_ref, m_ref, case_ref):
    hops = row_hop(sc, 0), row_hop(sc, 1)
    down, over, up, under = (
        ((hops[0] == h) | (hops[1] == h)).astype(jnp.int32) for h in (0, 1, 3, 4)
    )
    case_ref[0] = jnp.where(over + under == 2, 4, (down | up) + 2 * (over | under))
    for op in range(NDISP):
        m_ref[HOPS + op : HOPS + op + 1, :] = jnp.full((1, LANES), hops[op].astype(F32))
    m_ref[HOPS + 2 : HOPS + 3, :] = jnp.full((1, LANES), over.astype(F32))
    m_ref[HOPS + 3 :, :] = jnp.zeros((5, LANES), F32)
    here = 4 * (lax.axis_index("vec") // 2)
    lane = lane_of((1, LANES))
    for op in range(NMOM):
        part_x = ((mom[op, 0] * lax.axis_index("space")) & (slabs - 1)).astype(F32) / slabs
        part_z = ((mom[op, 2] * (lane & (NZ - 1))) & (NZ - 1)).astype(F32) / NZ
        for q in range(2):
            row = here + 2 * q + lane // NZ
            part_y = ((mom[op, 1] * row) & (NY - 1)).astype(F32) / NY
            angle = (part_x + part_y + part_z) * (2.0 * math.pi)
            at = PHASES + 4 * op + q
            m_ref[at : at + 1, :] = jnp.cos(angle)
            m_ref[at + 2 : at + 3, :] = jnp.sin(angle)
    block = lax.axis_index("vec") // 2
    low = lane_of((1, LANES)) < NZ
    for op in range(NDISP):
        hop = row_hop(sc, op)
        direction = lax.rem(hop, 3)

        def put(reim, row, col, q, value):
            m_ref[pl.ds(((op * 18 + reim * 9 + row * 3 + col) * 2) + q, 1), :] = value

        @pl.when(hop < 3)
        def _():
            for n in range(18):
                for q in range(2):
                    m_ref[pl.ds((op * 18 + n) * 2 + q, 1), :] = g_ref[
                        direction * 18 + n, pl.ds(2 * block + q, 1), :
                    ]

        def dagger(rows_of):
            for reim in range(2):
                for row in range(3):
                    for col in range(3):
                        n = reim * 9 + col * 3 + row
                        for q in range(2):
                            value = rows_of(n, q)
                            put(reim, row, col, q, -value if reim else value)

        @pl.when(hop == 3)
        def _():
            dagger(lambda n, q: behind_ref[12 * ROWS + 2 * n + q : 12 * ROWS + 2 * n + q + 1, :])

        @pl.when(hop == 4)
        def _():
            def rows_of(n, q):
                under = g_ref[18 + n, pl.ds(lax.rem(2 * block + q + ROWS - 1, ROWS), 1), :]
                here = g_ref[18 + n, pl.ds(2 * block + q, 1), :]
                return pltpu.roll(jnp.where(low, here, under), NZ, 1)

            dagger(rows_of)

        @pl.when(hop == 5)
        def _():
            dagger(lambda n, q: z_prev(g_ref[36 + n, pl.ds(2 * block + q, 1), :]))


def rows_of_block(ref, tile, odd):
    both = ref[:, 8 * tile : 8 * tile + 8, :].reshape(8, 2, 8, LANES)
    left, right = both[:, 0], both[:, 1]
    low = lax.broadcasted_iota(jnp.int32, left.shape, 1) < 4
    if odd:
        mixed = jnp.where(low, pltpu.roll(left, 4, 1), right)
    else:
        mixed = jnp.where(low, left, pltpu.roll(right, 4, 1))
    return mixed.reshape(64, LANES)


def split(x):
    high = x.astype(jnp.bfloat16)
    return high, (x - high.astype(F32)).astype(jnp.bfloat16)


def gram_body(
    scale, along_x, sides, own_ref, other_ref, ahead_ref, behind_ref, m_ref,
    out_ref, f_ref, n_ref, lhs, rhs,
):
    core = lax.rem(lax.axis_index("vec"), 2)

    def column(k, q):
        return slice((2 * k + q) * LANES, (2 * k + q + 1) * LANES)

    def put_lhs(op, k, q, value):
        high, rest = split(value)
        at = slice(64 * op, 64 * op + 64)
        lhs[0, at, column(k, q)] = high
        lhs[1, at, column(k, q)] = rest

    for q in range(2):
        for pair in range(3):
            tile = 3 * q + pair
            own = own_ref[:, 8 * tile : 8 * tile + 8, :]
            other = other_ref[:, 8 * tile : 8 * tile + 8, :]
            zero = jnp.where(core == 0, own, other)
            one = jnp.where(core == 0, other, own)
            low = lax.broadcasted_iota(jnp.int32, own.shape, 1) < 4
            even = jnp.where(low, zero, pltpu.roll(one, 4, 1)).reshape(128, LANES)
            odd = jnp.where(low, pltpu.roll(zero, 4, 1), one).reshape(128, LANES)
            for k, value in ((2 * pair, even), (2 * pair + 1, odd)):
                high, rest = split(value)
                for which, part in ((0, high), (1, rest)):
                    rhs[which, 0:128, column(k, q)] = part
                    if k < 3:
                        rhs[which, 128:256, column(k + 3, q)] = -part
                    else:
                        rhs[which, 128:256, column(k - 3, q)] = part
            for odd_one in (0, 1):
                f_ref[2 * pair + odd_one, q] = rows_of_block(own_ref, tile, odd_one)
    def phase(op, carry):
        for q in range(2):
            at = PHASES + 4 * op + q
            cosine, sine = m_ref[pl.ds(at, 1), :], m_ref[pl.ds(at + 2, 1), :]
            for c in range(3):
                re, im = f_ref[c, q], f_ref[3 + c, q]
                put_lhs(op, c, q, cosine * re + sine * im)
                put_lhs(op, 3 + c, q, cosine * im - sine * re)
        return carry

    for op in range(NMOM):
        phase(op, 0)
    low = lane_of((64, LANES)) < NZ
    def displace(op, carry):
        hop = jnp.max(m_ref[HOPS + op : HOPS + op + 1, :]).astype(jnp.int32)

        for which, ref in ((0, ahead_ref), (3, behind_ref)) if along_x else ():

            @pl.when(hop == which)
            def _():
                for k in range(6):
                    for q in range(2):
                        n_ref[k, q] = rows_of_block(ref, 3 * q + k // 2, k % 2)

        def edge(k, hop):
            if sides == 2:
                return rows_of_block(own_ref, 6 + k // 2, k % 2)
            packed = rows_of_block(own_ref, 6 + (k % 3) // 2, (k % 3) % 2)
            return packed if (k < 3) == (hop == 4) else pltpu.roll(packed, NZ, 1)

        for which in (1, 4) if sides else ():

            @pl.when(hop == which)
            def _():
                for k in range(6):
                    here, over = pltpu.roll(f_ref[k, 0], NZ, 1), pltpu.roll(f_ref[k, 1], NZ, 1)
                    if which == 1:
                        n_ref[k, 0] = jnp.where(low, here, over)
                        n_ref[k, 1] = jnp.where(low, over, edge(k, which))
                    else:
                        n_ref[k, 0] = jnp.where(low, edge(k, which), here)
                        n_ref[k, 1] = jnp.where(low, here, over)

        @pl.when(hop == 2)
        def _():
            for k in range(6):
                for q in range(2):
                    n_ref[k, q] = z_next(f_ref[k, q])

        @pl.when(hop == 5)
        def _():
            for k in range(6):
                for q in range(2):
                    n_ref[k, q] = z_prev(f_ref[k, q])

        for q in range(2):

            def link(reim, row, col):
                at = (op * 18 + reim * 9 + row * 3 + col) * 2 + q
                return m_ref[pl.ds(at, 1), :]

            moved = times(link, [n_ref[k, q] for k in range(6)])
            for k in range(6):
                put_lhs(NMOM + op, k, q, moved[k])
        return carry

    for op in range(NDISP):
        displace(op, 0)
    def dot(i, j):
        return lax.dot_general(
            lhs[i], rhs[j], (((1,), (1,)), ((), ())), preferred_element_type=F32
        )

    sums = dot(0, 0) + (dot(0, 1) + dot(1, 0))
    tiles = [
        sums[64 * op : 64 * op + 64, 128 * reim : 128 * reim + 128] * scale
        for reim in range(2)
        for op in range(4)
    ]
    group = lane_of((64, LANES)) // 16
    for bit in (4, 2, 1):
        clear = lax.rem(group // bit, 2) == 0
        for i in range(8):
            if i & bit == 0:
                a, b = tiles[i], tiles[i + bit]
                tiles[i] = jnp.where(clear, a, pltpu.roll(b, 16 * bit, 1))
                tiles[i + bit] = jnp.where(clear, pltpu.roll(a, LANES - 16 * bit, 1), b)
    for slab in range(8):
        out_ref[slab] = tiles[slab]


def finish_body(part_ref, out_ref):
    parts = [part_ref[8 * i : 8 * i + 8, :] for i in range(64)]
    while len(parts) > 1:
        parts = [a + b for a, b in zip(parts[::2], parts[1::2])]
    total = parts[0] + pltpu.roll(parts[0], 4, 0)
    for t in range(8):
        moved = total if t == 0 else pltpu.roll(total, LANES - 16 * t, 1)
        out_ref[t] = moved[:4, :16]


def local(slabs, vecs, vectors, gauge_links, momenta, displacements):
    field_bytes = 24 * ROWS * LANES * 4
    field = vectors.reshape(24, ROWS, LANES)
    gauge = gauge_links.reshape(54, ROWS, LANES)
    up = [(i, (i + 1) % slabs) for i in range(slabs)]
    down = [(i, (i - 1) % slabs) for i in range(slabs)]
    partner = [(i, i ^ 1) for i in range(vecs)]
    cores = [[2 * i + c for i in range(vecs // 2)] for c in range(2)]
    alike = [[2 * i + c for i in range(slabs * vecs // 2)] for c in range(2)]

    half = struct(12, ROWS, LANES)
    rows = struct(12 * ROWS, LANES)
    va, vb, wa, wb = call(
        start_body,
        [half, half, rows, rows],
        "hh",
        scratch=[VMEM((18, ROWS, LANES), F32), pltpu.SemaphoreType.DMA((18,))],
        flops=3 << 20,
        nbytes=3 * field_bytes,
        room=63400,
    )(field, gauge)
    inner = call(inner_body, half, "vv", flops=6 << 20, nbytes=3 * field_bytes)

    def step(links_too, *operands):
        w = struct(12 * ROWS + 40, LANES) if links_too else rows
        body = functools.partial(first_body, links_too)
        return call(body, [half, w], "vvvx", flops=3 << 20, nbytes=3 * field_bytes)(*operands)

    def exchange(v, w):
        return lax.ppermute(v, "space", down), lax.ppermute(w, "space", up)

    aheada, behinda = exchange(va, wa)
    aheadb, behindb = exchange(vb, wb)
    firsta, wa = step(True, inner(va, gauge), aheada, behinda, gauge)
    ahead2a, behind2a = exchange(firsta, wa)
    firstb, wb = step(False, inner(vb, gauge), aheadb, behindb, gauge)
    ahead2b, behind2b = exchange(firstb, wb)
    acca, accb = inner(firsta, gauge), inner(firstb, gauge)
    table, case = call(
        functools.partial(table_body, slabs),
        [struct(HOPS + 8, LANES), jax.ShapeDtypeStruct((1,), jnp.int32)],
        "ssvv",
        flops=1 << 20,
        nbytes=4 * field_bytes,
    )(displacements, momenta, gauge, behind2a)
    acca, accb, table, case = lax.optimization_barrier((acca, accb, table, case))
    scale = 1.0 / math.sqrt(3 * slabs * NY * NZ)

    def partial_sums(along_x, sides, fields, gauge, table):
        cut = call(
            functools.partial(second_body, sides),
            struct(16, (48, 64, 72)[sides], LANES),
            "vvvvvvvvvx",
            scratch=[VMEM((24 * ROWS, LANES), F32)] * 2,
            flops=6 << 20,
            nbytes=7 * field_bytes,
        )(table, *fields, gauge)
        own = lax.all_to_all(cut, "vec", 0, 0, axis_index_groups=cores)
        bulk = own[:, :48]
        ahead = lax.ppermute(bulk, "space", down) if along_x else bulk
        behind = lax.ppermute(bulk, "space", up) if along_x else bulk
        other = lax.ppermute(bulk, "vec", partner)
        return call(
            functools.partial(gram_body, scale, along_x, sides),
            struct(slabs, 64, LANES),
            "vvvvv",
            scratch=[VMEM((6, 2, 64, LANES), F32)] * 2
            + [VMEM((2, 256, 12 * LANES), jnp.bfloat16)] * 2,
            room=16384,
            flops=600 << 20,
            nbytes=6 * field_bytes,
        )(own, other, ahead, behind, table)

    sums = lax.switch(
        case[0],
        [functools.partial(partial_sums, *case_of) for case_of in CASES],
        (acca, ahead2a, behind2a, va, accb, ahead2b, behind2b, vb),
        gauge,
        table,
    )
    sums = sums.reshape(slabs * vecs // 2, 4, LANES)
    parts = lax.all_to_all(sums, ("space", "vec"), 0, 0, axis_index_groups=alike)
    out = call(finish_body, struct(8, 4, 16), "v")(parts.reshape(512, LANES))
    return out.reshape(2, 4, 4, 16)


def solution(mesh):
    placed = (
        P(None, None, "vec", "space", None),
        P(None, None, None, None, "space", None),
        P(),
        P(),
    )
    body = functools.partial(local, mesh.shape["space"], mesh.shape["vec"])
    return jax.shard_map(
        body, mesh=mesh, in_specs=placed, out_specs=P(None, None, "vec", "space"), check_vma=False
    )
```

```python
import functools
import math

import jax
import jax.numpy as jnp
from jax import lax
from jax.experimental import pallas as pl
from jax.experimental.pallas import tpu as pltpu
from jax.sharding import PartitionSpec as P

NY = 64
NZ = 64
NMOM = 2
NDISP = 2
ROWS = 32
LANES = 128
CASES = ((False, 0), (True, 0), (False, 1), (True, 1), (False, 2))
PHASES = 36 * NDISP
HOPS = PHASES + 4 * NMOM
VMEM = pltpu.VMEM
F32 = jnp.float32


LINKS = pl.BlockSpec((18, ROWS, LANES), lambda i: (0, 0, 0))


SMEM_BLOCK = pl.BlockSpec(memory_space=pltpu.SMEM)


def call(body, out_shape, ins, scratch=(), flops=0, nbytes=0, room=8192):
    kinds = {
        "s": SMEM_BLOCK,
        "x": LINKS,
        "v": pl.BlockSpec(memory_space=VMEM),
        "h": pl.BlockSpec(memory_space=pl.ANY),
    }
    specs = [kinds[letter] for letter in ins]
    many = isinstance(out_shape, (list, tuple))
    return pl.pallas_call(
        body,
        out_shape=out_shape,
        grid=(1,) if "x" in ins else (),
        in_specs=specs,
        out_specs=[
            pl.BlockSpec(memory_space=VMEM) if each.dtype != jnp.int32 else SMEM_BLOCK
            for each in out_shape
        ]
        if many
        else pl.BlockSpec(memory_space=VMEM),
        scratch_shapes=list(scratch),
        cost_estimate=pl.CostEstimate(flops=flops, bytes_accessed=nbytes, transcendentals=0),
        compiler_params=pltpu.CompilerParams(vmem_limit_bytes=room << 10),
    )


def struct(*shape):
    return jax.ShapeDtypeStruct(shape, F32)


def times(link, field):
    out = []
    for i in range(3):
        re = im = None
        for j in range(3):
            a, b = link(0, i, j), link(1, i, j)
            x, y = field[j], field[3 + j]
            re_j, im_j = a * x - b * y, a * y + b * x
            re = re_j if re is None else re + re_j
            im = im_j if im is None else im + im_j
        out.append((re, im))
    return [o[0] for o in out] + [o[1] for o in out]


def times_dagger(link, field):
    out = []
    for i in range(3):
        re = im = None
        for j in range(3):
            a, b = link(0, j, i), link(1, j, i)
            x, y = field[j], field[3 + j]
            re_j, im_j = a * x + b * y, a * y - b * x
            re = re_j if re is None else re + re_j
            im = im_j if im is None else im + im_j
        out.append((re, im))
    return [o[0] for o in out] + [o[1] for o in out]


def lane_of(shape):
    return lax.broadcasted_iota(jnp.int32, shape, len(shape) - 1)


def z_next(x):
    axis = x.ndim - 1
    end = lane_of(x.shape) % NZ == NZ - 1
    return jnp.where(end, pltpu.roll(x, NZ - 1, axis), pltpu.roll(x, LANES - 1, axis))


def z_prev(x):
    axis = x.ndim - 1
    start = lane_of(x.shape) % NZ == 0
    return jnp.where(start, pltpu.roll(x, LANES - NZ + 1, axis), pltpu.roll(x, 1, axis))


def y_next(x):
    half = pltpu.roll(x, NZ, 1)
    return jnp.where(lane_of(x.shape) < NZ, half, pltpu.roll(half, ROWS - 1, 0))


def y_prev(x):
    half = pltpu.roll(x, NZ, 1)
    return jnp.where(lane_of(x.shape) < NZ, pltpu.roll(half, 1, 0), half)


def plane_link(g_ref, direction):
    return lambda reim, row, col: g_ref[direction * 18 + reim * 9 + row * 3 + col]


def start_body(v_hbm, g_hbm, va_ref, vb_ref, wa_ref, wb_ref, g_ref, sems):
    early, late = [], []
    for i in range(6):
        for half, v_ref, group in ((0, va_ref, early), (1, vb_ref, late)):
            group.append(
                pltpu.make_async_copy(
                    v_hbm.at[pl.ds(4 * i + 2 * half, 2)],
                    v_ref.at[pl.ds(2 * i, 2)],
                    sems.at[2 * i + half],
                )
            )
        early.append(
            pltpu.make_async_copy(
                g_hbm.at[pl.ds(3 * i, 3)], g_ref.at[pl.ds(3 * i, 3)], sems.at[12 + i]
            )
        )
    for copy in early + late:
        copy.start()
    link = plane_link(g_ref, 0)
    for v_ref, w_ref, group in ((va_ref, wa_ref, early), (vb_ref, wb_ref, late)):
        for copy in group:
            copy.wait()
        for n in range(2):
            out = times_dagger(link, [v_ref[2 * k + n] for k in range(6)])
            for k in range(6):
                w_ref[(2 * k + n) * ROWS : (2 * k + n + 1) * ROWS, :] = out[k]


def inner_body(v_ref, g_ref, acc_ref):
    link_y, link_z = plane_link(g_ref, 1), plane_link(g_ref, 2)

    def one(n, carry):
        field = [v_ref[2 * k + n] for k in range(6)]
        total = times(link_y, [y_next(x) for x in field])
        for part in (
            [y_prev(x) for x in times_dagger(link_y, field)],
            times(link_z, [z_next(x) for x in field]),
            [z_prev(x) for x in times_dagger(link_z, field)],
        ):
            total = [a + b for a, b in zip(total, part)]
        for k in range(6):
            acc_ref[2 * k + n] = total[k]
        return carry

    lax.fori_loop(0, 2, one, 0)


def summed(n, acc_ref, ahead_ref, behind_ref, link):
    hop = times(link, [ahead_ref[2 * k + n] for k in range(6)])
    return [
        acc_ref[2 * k + n] + hop[k] + behind_ref[pl.ds((2 * k + n) * ROWS, ROWS), :]
        for k in range(6)
    ]


def first_body(links_too, acc_ref, ahead_ref, behind_ref, g_ref, first_ref, w_ref):
    link = plane_link(g_ref, 0)

    def one(n, carry):
        first = [x / -6.0 for x in summed(n, acc_ref, ahead_ref, behind_ref, link)]
        out = times_dagger(link, first)
        for k in range(6):
            first_ref[2 * k + n] = first[k]
            w_ref[pl.ds((2 * k + n) * ROWS, ROWS), :] = out[k]
        return carry

    lax.fori_loop(0, 2, one, 0)
    if links_too:
        block = lax.axis_index("vec") // 2
        for n in range(18):
            at = 12 * ROWS + 2 * n
            w_ref[at : at + 2, :] = g_ref[n, pl.ds(2 * block, 2), :]
        w_ref[12 * ROWS + 36 :, :] = jnp.zeros((4, LANES), F32)


def filter_half(half, acc_ref, ahead_ref, behind_ref, v_ref, link, f_ref, half_ref):
    def one(n, carry):
        total = summed(n, acc_ref, ahead_ref, behind_ref, link)
        for k in range(6):
            f = total[k] / -3.0 - v_ref[2 * k + n]
            at = pl.ds((4 * k + 2 * half + n) * ROWS, ROWS)
            f_ref[at, :] = f
            if half_ref is not None:
                half_ref[at, :] = pltpu.roll(f, NZ, 1)
        return carry

    lax.fori_loop(0, 2, one, 0)


def row_hop(sc, op):
    return lax.rem(sc[op] + 3, 6)


def second_body(
    sides, m_ref, acca, aheada, behinda, va, accb, aheadb, behindb, vb, g_ref,
    out_ref, f_ref, half_ref,
):
    link = plane_link(g_ref, 0)
    rolled = half_ref if sides else None
    filter_half(0, acca, aheada, behinda, va, link, f_ref, rolled)
    filter_half(1, accb, aheadb, behindb, vb, link, f_ref, rolled)

    def cut(block, edge):
        for q in range(2):
            out_ref[block, 24 * q : 24 * q + 24, :] = f_ref[pl.ds(2 * block + q, 24, ROWS), :]
        under, over = (2 * block - 1) % ROWS, (2 * block + 2) % ROWS
        if edge is None:
            return
        if edge == "two":
            low = lane_of((24, LANES)) < NZ
            both = half_ref[pl.ds(under, 24, ROWS), :], half_ref[pl.ds(over, 24, ROWS), :]
            out_ref[block, 48:72, :] = jnp.where(low, *both)
            return
        low = lane_of((12, LANES)) < NZ

        def rows(ref, at):
            return ref[pl.ds(at, 12, ROWS), :]

        above = jnp.where(low, rows(f_ref, over), rows(half_ref, over + 12 * ROWS))
        below = jnp.where(low, rows(half_ref, under), rows(f_ref, under + 12 * ROWS))
        out_ref[block, 48:60, :] = jnp.where(m_ref[HOPS + 2 : HOPS + 3, :] > 0.5, above, below)
        out_ref[block, 60:64, :] = jnp.zeros((4, LANES), F32)

    for block in range(16):
        cut(block, (None, "one", "two")[sides])


def table_body(slabs, sc, mom, g_ref, behind_ref, m_ref, case_ref):
    hops = row_hop(sc, 0), row_hop(sc, 1)
    down, over, up, under = (
        ((hops[0] == h) | (hops[1] == h)).astype(jnp.int32) for h in (0, 1, 3, 4)
    )
    case_ref[0] = jnp.where(over + under == 2, 4, (down | up) + 2 * (over | under))
    for op in range(NDISP):
        m_ref[HOPS + op : HOPS + op + 1, :] = jnp.full((1, LANES), hops[op].astype(F32))
    m_ref[HOPS + 2 : HOPS + 3, :] = jnp.full((1, LANES), over.astype(F32))
    m_ref[HOPS + 3 :, :] = jnp.zeros((5, LANES), F32)
    here = 4 * (lax.axis_index("vec") // 2)
    lane = lane_of((1, LANES))
    for op in range(NMOM):
        part_x = ((mom[op, 0] * lax.axis_index("space")) & (slabs - 1)).astype(F32) / slabs
        part_z = ((mom[op, 2] * (lane & (NZ - 1))) & (NZ - 1)).astype(F32) / NZ
        for q in range(2):
            row = here + 2 * q + lane // NZ
            part_y = ((mom[op, 1] * row) & (NY - 1)).astype(F32) / NY
            angle = (part_x + part_y + part_z) * (2.0 * math.pi)
            at = PHASES + 4 * op + q
            m_ref[at : at + 1, :] = jnp.cos(angle)
            m_ref[at + 2 : at + 3, :] = jnp.sin(angle)
    block = lax.axis_index("vec") // 2
    low = lane_of((1, LANES)) < NZ
    for op in range(NDISP):
        hop = row_hop(sc, op)
        direction = lax.rem(hop, 3)

        def put(reim, row, col, q, value):
            m_ref[pl.ds(((op * 18 + reim * 9 + row * 3 + col) * 2) + q, 1), :] = value

        @pl.when(hop < 3)
        def _():
            for n in range(18):
                for q in range(2):
                    m_ref[pl.ds((op * 18 + n) * 2 + q, 1), :] = g_ref[
                        direction * 18 + n, pl.ds(2 * block + q, 1), :
                    ]

        def dagger(rows_of):
            for reim in range(2):
                for row in range(3):
                    for col in range(3):
                        n = reim * 9 + col * 3 + row
                        for q in range(2):
                            value = rows_of(n, q)
                            put(reim, row, col, q, -value if reim else value)

        @pl.when(hop == 3)
        def _():
            dagger(lambda n, q: behind_ref[12 * ROWS + 2 * n + q : 12 * ROWS + 2 * n + q + 1, :])

        @pl.when(hop == 4)
        def _():
            def rows_of(n, q):
                under = g_ref[18 + n, pl.ds(lax.rem(2 * block + q + ROWS - 1, ROWS), 1), :]
                here = g_ref[18 + n, pl.ds(2 * block + q, 1), :]
                return pltpu.roll(jnp.where(low, here, under), NZ, 1)

            dagger(rows_of)

        @pl.when(hop == 5)
        def _():
            dagger(lambda n, q: z_prev(g_ref[36 + n, pl.ds(2 * block + q, 1), :]))


def rows_of_block(ref, tile, odd):
    both = ref[:, 8 * tile : 8 * tile + 8, :].reshape(8, 2, 8, LANES)
    left, right = both[:, 0], both[:, 1]
    low = lax.broadcasted_iota(jnp.int32, left.shape, 1) < 4
    if odd:
        mixed = jnp.where(low, pltpu.roll(left, 4, 1), right)
    else:
        mixed = jnp.where(low, left, pltpu.roll(right, 4, 1))
    return mixed.reshape(64, LANES)


def split(x):
    high = x.astype(jnp.bfloat16)
    return high, (x - high.astype(F32)).astype(jnp.bfloat16)


def gram_body(
    scale, along_x, sides, own_ref, other_ref, ahead_ref, behind_ref, m_ref,
    out_ref, f_ref, n_ref, lhs, rhs,
):
    core = lax.rem(lax.axis_index("vec"), 2)

    def column(k, q):
        return slice((2 * k + q) * LANES, (2 * k + q + 1) * LANES)

    def put_lhs(op, k, q, value):
        high, rest = split(value)
        at = slice(64 * op, 64 * op + 64)
        lhs[0, at, column(k, q)] = high
        lhs[1, at, column(k, q)] = rest

    for q in range(2):
        for pair in range(3):
            tile = 3 * q + pair
            own = own_ref[:, 8 * tile : 8 * tile + 8, :]
            other = other_ref[:, 8 * tile : 8 * tile + 8, :]
            zero = jnp.where(core == 0, own, other)
            one = jnp.where(core == 0, other, own)
            low = lax.broadcasted_iota(jnp.int32, own.shape, 1) < 4
            even = jnp.where(low, zero, pltpu.roll(one, 4, 1)).reshape(128, LANES)
            odd = jnp.where(low, pltpu.roll(zero, 4, 1), one).reshape(128, LANES)
            for k, value in ((2 * pair, even), (2 * pair + 1, odd)):
                high, rest = split(value)
                for which, part in ((0, high), (1, rest)):
                    rhs[which, 0:128, column(k, q)] = part
                    if k < 3:
                        rhs[which, 128:256, column(k + 3, q)] = -part
                    else:
                        rhs[which, 128:256, column(k - 3, q)] = part
            for odd_one in (0, 1):
                f_ref[2 * pair + odd_one, q] = rows_of_block(own_ref, tile, odd_one)
    def phase(op, carry):
        for q in range(2):
            at = PHASES + 4 * op + q
            cosine, sine = m_ref[pl.ds(at, 1), :], m_ref[pl.ds(at + 2, 1), :]
            for c in range(3):
                re, im = f_ref[c, q], f_ref[3 + c, q]
                put_lhs(op, c, q, cosine * re + sine * im)
                put_lhs(op, 3 + c, q, cosine * im - sine * re)
        return carry

    for op in range(NMOM):
        phase(op, 0)
    low = lane_of((64, LANES)) < NZ
    def displace(op, carry):
        hop = jnp.max(m_ref[HOPS + op : HOPS + op + 1, :]).astype(jnp.int32)

        for which, ref in ((0, ahead_ref), (3, behind_ref)) if along_x else ():

            @pl.when(hop == which)
            def _():
                for k in range(6):
                    for q in range(2):
                        n_ref[k, q] = rows_of_block(ref, 3 * q + k // 2, k % 2)

        def edge(k, hop):
            if sides == 2:
                return rows_of_block(own_ref, 6 + k // 2, k % 2)
            packed = rows_of_block(own_ref, 6 + (k % 3) // 2, (k % 3) % 2)
            return packed if (k < 3) == (hop == 4) else pltpu.roll(packed, NZ, 1)

        for which in (1, 4) if sides else ():

            @pl.when(hop == which)
            def _():
                for k in range(6):
                    here, over = pltpu.roll(f_ref[k, 0], NZ, 1), pltpu.roll(f_ref[k, 1], NZ, 1)
                    if which == 1:
                        n_ref[k, 0] = jnp.where(low, here, over)
                        n_ref[k, 1] = jnp.where(low, over, edge(k, which))
                    else:
                        n_ref[k, 0] = jnp.where(low, edge(k, which), here)
                        n_ref[k, 1] = jnp.where(low, here, over)

        @pl.when(hop == 2)
        def _():
            for k in range(6):
                for q in range(2):
                    n_ref[k, q] = z_next(f_ref[k, q])

        @pl.when(hop == 5)
        def _():
            for k in range(6):
                for q in range(2):
                    n_ref[k, q] = z_prev(f_ref[k, q])

        for q in range(2):

            def link(reim, row, col):
                at = (op * 18 + reim * 9 + row * 3 + col) * 2 + q
                return m_ref[pl.ds(at, 1), :]

            moved = times(link, [n_ref[k, q] for k in range(6)])
            for k in range(6):
                put_lhs(NMOM + op, k, q, moved[k])
        return carry

    for op in range(NDISP):
        displace(op, 0)
    def dot(i, j):
        return lax.dot_general(
            lhs[i], rhs[j], (((1,), (1,)), ((), ())), preferred_element_type=F32
        )

    sums = dot(0, 0) + (dot(0, 1) + dot(1, 0))
    tiles = [
        sums[64 * op : 64 * op + 64, 128 * reim : 128 * reim + 128] * scale
        for reim in range(2)
        for op in range(4)
    ]
    group = lane_of((64, LANES)) // 16
    for bit in (4, 2, 1):
        clear = lax.rem(group // bit, 2) == 0
        for i in range(8):
            if i & bit == 0:
                a, b = tiles[i], tiles[i + bit]
                tiles[i] = jnp.where(clear, a, pltpu.roll(b, 16 * bit, 1))
                tiles[i + bit] = jnp.where(clear, pltpu.roll(a, LANES - 16 * bit, 1), b)
    for slab in range(8):
        out_ref[slab] = tiles[slab]


def finish_body(part_ref, out_ref):
    parts = [part_ref[8 * i : 8 * i + 8, :] for i in range(64)]
    while len(parts) > 1:
        parts = [a + b for a, b in zip(parts[::2], parts[1::2])]
    total = parts[0] + pltpu.roll(parts[0], 4, 0)
    for t in range(8):
        moved = total if t == 0 else pltpu.roll(total, LANES - 16 * t, 1)
        out_ref[t] = moved[:4, :16]


def local(slabs, vecs, vectors, gauge_links, momenta, displacements):
    field_bytes = 24 * ROWS * LANES * 4
    field = vectors.reshape(24, ROWS, LANES)
    gauge = gauge_links.reshape(54, ROWS, LANES)
    up = [(i, (i + 1) % slabs) for i in range(slabs)]
    down = [(i, (i - 1) % slabs) for i in range(slabs)]
    partner = [(i, i ^ 1) for i in range(vecs)]
    cores = [[2 * i + c for i in range(vecs // 2)] for c in range(2)]
    alike = [[2 * i + c for i in range(slabs * vecs // 2)] for c in range(2)]

    half = struct(12, ROWS, LANES)
    rows = struct(12 * ROWS, LANES)
    va, vb, wa, wb = call(
        start_body,
        [half, half, rows, rows],
        "hh",
        scratch=[VMEM((18, ROWS, LANES), F32), pltpu.SemaphoreType.DMA((18,))],
        flops=3 << 20,
        nbytes=3 * field_bytes,
        room=63400,
    )(field, gauge)
    inner = call(inner_body, half, "vv", flops=6 << 20, nbytes=3 * field_bytes)

    def step(links_too, *operands):
        w = struct(12 * ROWS + 40, LANES) if links_too else rows
        body = functools.partial(first_body, links_too)
        return call(body, [half, w], "vvvx", flops=3 << 20, nbytes=3 * field_bytes)(*operands)

    def exchange(v, w):
        return lax.ppermute(v, "space", down), lax.ppermute(w, "space", up)

    aheada, behinda = exchange(va, wa)
    aheadb, behindb = exchange(vb, wb)
    firsta, wa = step(True, inner(va, gauge), aheada, behinda, gauge)
    ahead2a, behind2a = exchange(firsta, wa)
    firstb, wb = step(False, inner(vb, gauge), aheadb, behindb, gauge)
    ahead2b, behind2b = exchange(firstb, wb)
    acca, accb = inner(firsta, gauge), inner(firstb, gauge)
    table, case = call(
        functools.partial(table_body, slabs),
        [struct(HOPS + 8, LANES), jax.ShapeDtypeStruct((1,), jnp.int32)],
        "ssvv",
        flops=1 << 20,
        nbytes=4 * field_bytes,
    )(displacements, momenta, gauge, behind2a)
    acca, accb, table, case = lax.optimization_barrier((acca, accb, table, case))
    scale = 1.0 / math.sqrt(3 * slabs * NY * NZ)

    def partial_sums(along_x, sides, fields, gauge, table):
        cut = call(
            functools.partial(second_body, sides),
            struct(16, (48, 64, 72)[sides], LANES),
            "vvvvvvvvvx",
            scratch=[VMEM((24 * ROWS, LANES), F32)] * 2,
            flops=6 << 20,
            nbytes=7 * field_bytes,
        )(table, *fields, gauge)
        own = lax.all_to_all(cut, "vec", 0, 0, axis_index_groups=cores)
        bulk = own[:, :48]
        ahead = lax.ppermute(bulk, "space", down) if along_x else bulk
        behind = lax.ppermute(bulk, "space", up) if along_x else bulk
        other = lax.ppermute(bulk, "vec", partner)
        return call(
            functools.partial(gram_body, scale, along_x, sides),
            struct(slabs, 64, LANES),
            "vvvvv",
            scratch=[VMEM((6, 2, 64, LANES), F32)] * 2
            + [VMEM((2, 256, 12 * LANES), jnp.bfloat16)] * 2,
            room=16384,
            flops=600 << 20,
            nbytes=6 * field_bytes,
        )(own, other, ahead, behind, table)

    sums = lax.switch(
        case[0],
        [functools.partial(partial_sums, *case_of) for case_of in CASES],
        (acca, ahead2a, behind2a, va, accb, ahead2b, behind2b, vb),
        gauge,
        table,
    )
    sums = sums.reshape(slabs * vecs // 2, 4, LANES)
    parts = lax.all_to_all(sums, ("space", "vec"), 0, 0, axis_index_groups=alike)
    out = call(finish_body, struct(8, 4, 16), "v")(parts.reshape(512, LANES))
    return out.reshape(2, 4, 4, 16)


def solution(mesh):
    placed = (
        P(None, None, "vec", "space", None),
        P(None, None, None, None, "space", None),
        P(),
        P(),
    )
    body = functools.partial(local, mesh.shape["space"], mesh.shape["vec"])
    return jax.shard_map(
        body, mesh=mesh, in_specs=placed, out_specs=P(None, None, "vec", "space"), check_vma=False
    )
```
